32 devices in a mesh: tower: 4 (over y, x), shard: 8 (over z, core).
Axes of the slice: x: 2, y: 2, z: 4, core: 2. Of those that a mesh axis runs over, the one named last changes fastest.
Arguments:
- pooled: bfloat16 [4, 3072, 48, 128], P('tower', None, 'shard'), may hold values from -6 to 6
- cross_down: bfloat16 [4, 2, 4096, 512], P('tower', None, 'shard'), may hold values from -0.09375 to 0.09375
- cross_up: bfloat16 [4, 2, 512, 4096], P('tower', None, None, 'shard'), may hold values from -0.25 to 0.25
- cross_bias: bfloat16 [4, 2, 4096], P('tower'), may hold values from -3 to 3
- comp_weight: bfloat16 [4, 4096, 256], P('tower', 'shard'), may hold values from -0.09375 to 0.09375
- comp_bias: bfloat16 [4, 256], P('tower'), may hold values from -3 to 3
- over_weight: bfloat16 [1024, 1024], P('tower', 'shard'), may hold values from -0.1875 to 0.1875
- over_bias: bfloat16 [1024], replicated, may hold values from -3 to 3
- table_tower: int32 [128], replicated, may hold values from 0 to 3, as said below
- table_owner: int32 [128], replicated, may hold values from 0 to 7, as said below
Outputs:
- scores: bfloat16 [8, 384, 1024], P('shard', 'tower')
The draws below stay inside these ranges and needn't reach their ends.
Inputs may be any that keep to these rules, and one draw needn't show every extreme that they name: `table_tower`: each value names exactly 32 tables. `table_owner`: among the tables of one tower no value is named by more than 6 tables, and in every tower some value is named by exactly 6.
All inputs are finite; a program needn't handle non-finite values.
Results may differ from the reference program's by a relative error of at most 0.014.
Values may be sent and summed in bfloat16 or wider, within the bound.
A program may use at most 128 MiB of HBM per device.

```python
import jax
import jax.numpy as jnp
from jax import lax

EMB = 128
TPT = 32
RANK = 512
CMP = 256
OUT = 1024
LAYERS = 2
SMP_DEV = 384
TOWERS = 4
TABLES = 128
F = 4096
CAT = 1024
TAB_MOST = 6
SLOTS = 48
BATCH = 3072
N_TOWER = 4
N_SHARD = 8


def placement_order(key):
    return jax.random.permutation(jax.random.fold_in(key, 11), TABLES).astype(jnp.int32)


def draw_table_tower(key, part):
    order = placement_order(key)
    return (order // TPT).astype(jnp.int32)


def draw_table_owner(key, part):
    order = placement_order(key)
    tower_of = order // TPT
    position = order % TPT

    def one_tower(tower_key):
        first_key, second_key = jax.random.split(tower_key)
        full_owner = jax.random.randint(first_key, (), 0, SLOTS // TAB_MOST)
        slot_ids = jnp.arange(SLOTS, dtype=jnp.int32)
        owners = slot_ids // TAB_MOST
        scores = jax.random.permutation(second_key, SLOTS).astype(jnp.int32)
        scores = jnp.where(owners == full_owner, slot_ids % TAB_MOST - TAB_MOST, scores)
        chosen = jnp.argsort(scores)[:TPT]
        return (chosen // TAB_MOST).astype(jnp.int32)
    tower_keys = jax.random.split(jax.random.fold_in(key, 23), TOWERS)
    assigned = jax.vmap(one_tower)(tower_keys)
    return assigned[tower_of, position].astype(jnp.int32)


def level_of(key, shape, cuts, smallest, top_value):
    def one(dim, blocks):
        steps = jax.random.uniform(jax.random.fold_in(jax.random.fold_in(key, 6), dim), (blocks,), jnp.float32, smallest / len(cuts), top_value / len(cuts))
        return jnp.repeat(jnp.exp(steps), shape[dim] // blocks).reshape((-1,) + (1,) * (len(shape) - dim - 1))

    factor_of = one(*cuts[0])
    for cut in cuts[1:]:
        factor_of = factor_of * one(*cut)
    return factor_of


def noise(stream_key, extent, width, reach, cuts=(), kind=jnp.bfloat16):
    array = width * jax.random.normal(stream_key, extent, jnp.float32)
    if cuts:
        array = array * level_of(stream_key, extent, cuts, -0.22, 0.18)
    return jnp.clip(array, -reach, reach).astype(kind)


def setup_inputs(seed: int = 0) -> dict:
    arg_keys = jax.random.split(jax.random.key(seed), 11)
    return {
        "pooled": noise(arg_keys[0], (TOWERS, BATCH, SLOTS, EMB), 1.0, 6.0, ((0, 4), (2, 8))),
        "cross_down": noise(arg_keys[1], (TOWERS, LAYERS, F, RANK), F ** -0.5, 0.09375, ((0, 4), (2, 8))),
        "cross_up": noise(arg_keys[2], (TOWERS, LAYERS, RANK, F), RANK ** -0.5, 0.25, ((0, 4), (3, 8))),
        "cross_bias": noise(arg_keys[3], (TOWERS, LAYERS, F), 0.5, 3.0, ((0, 4),)),
        "comp_weight": noise(arg_keys[4], (TOWERS, F, CMP), F ** -0.5, 0.09375, ((0, 4), (1, 8))),
        "comp_bias": noise(arg_keys[5], (TOWERS, CMP), 0.5, 3.0, ((0, 4),)),
        "over_weight": noise(arg_keys[6], (CAT, OUT), CAT ** -0.5, 0.1875, ((0, 4), (1, 8))),
        "over_bias": noise(arg_keys[7], (OUT,), 0.5, 3.0),
        "table_tower": draw_table_tower(jax.random.fold_in(arg_keys[10], 71), 0),
        "table_owner": draw_table_owner(jax.random.fold_in(arg_keys[10], 71), 0),
    }


def slot_order(table_tower, table_owner, tower_id):
    index = jnp.arange(TABLES, dtype=jnp.int32)
    inside = table_tower == tower_id
    earlier = index[None, :] < index[:, None]
    before = inside[None, :] & earlier
    position_in = jnp.sum(before.astype(jnp.int32), axis=1).astype(jnp.int32)
    same_owner = table_owner[None, :] == table_owner[:, None]
    own_slot = jnp.sum((before & same_owner).astype(jnp.int32), axis=1).astype(jnp.int32)
    wanted = (table_owner * TAB_MOST + own_slot).astype(jnp.int32)
    picked = inside[None, :] & (position_in[None, :] == jnp.arange(TPT, dtype=jnp.int32)[:, None])
    return jnp.sum(jnp.where(picked, wanted[None, :], 0), axis=1).astype(jnp.int32)


def reference(pooled, cross_down, cross_up, cross_bias, comp_weight, comp_bias, over_weight, over_bias, table_tower, table_owner):
    def one_tower(tower_id):
        wanted = slot_order(table_tower, table_owner, tower_id)
        tables = jnp.take(pooled[tower_id], wanted, axis=1)
        base = tables.reshape(BATCH, F)
        state = base
        for section_index in range(LAYERS):
            lowered = jnp.dot(state, cross_down[tower_id, section_index], preferred_element_type=jnp.float32).astype(jnp.bfloat16)
            raised = jnp.dot(lowered, cross_up[tower_id, section_index], preferred_element_type=jnp.float32)
            state = (base.astype(jnp.float32) * (raised + cross_bias[tower_id, section_index].astype(jnp.float32)) + state.astype(jnp.float32)).astype(jnp.bfloat16)
        squeezed = jnp.dot(state, comp_weight[tower_id], preferred_element_type=jnp.float32) + comp_bias[tower_id].astype(jnp.float32)
        return squeezed.astype(jnp.bfloat16)

    towers_out = lax.map(one_tower, jnp.arange(N_TOWER, dtype=jnp.int32))
    joined = jnp.transpose(towers_out, (1, 0, 2)).reshape(BATCH, CAT)
    mixed = jnp.dot(joined, over_weight, preferred_element_type=jnp.float32) + over_bias.astype(jnp.float32)
    return jax.nn.relu(mixed).astype(jnp.bfloat16).reshape(N_SHARD, SMP_DEV, OUT)
```

```python
import jax
import jax.numpy as jnp
from jax import lax
from jax.experimental import pallas as pl
from jax.experimental.pallas import tpu as pltpu
from jax.sharding import PartitionSpec as P

MESH = pl.DeviceIdType.MESH
CORES = 2
SIDE = 2
CHUNKS = 6
BF16, F32 = jnp.bfloat16, jnp.float32


def slot_order(table_tower, table_owner, tower_id, per_tower, slot_most):
    table_count = table_tower.shape[0]
    index = jnp.arange(table_count, dtype=jnp.int32)
    inside = table_tower == tower_id
    earlier = index[None, :] < index[:, None]
    before = inside[None, :] & earlier
    position_in = jnp.sum(before.astype(jnp.int32), axis=1)
    same_owner = table_owner[None, :] == table_owner[:, None]
    own_slot = jnp.sum((before & same_owner).astype(jnp.int32), axis=1)
    wanted = table_owner * slot_most + own_slot
    picked = inside[None, :] & (
        position_in[None, :] == jnp.arange(per_tower, dtype=jnp.int32)[:, None]
    )
    return jnp.sum(jnp.where(picked, wanted[None, :], 0), axis=1)


def on_device(
    pooled,
    cross_down,
    cross_up,
    cross_bias,
    comp_weight,
    comp_bias,
    over_weight,
    over_bias,
    table_tower,
    table_owner,
):
    tower_id = lax.axis_index("tower")
    slot_most = pooled.shape[2]
    emb_width = pooled.shape[3]
    feature_count = cross_up.shape[3] * lax.axis_size("shard")
    per_tower = feature_count // emb_width
    received = lax.all_to_all(pooled, "shard", split_axis=1, concat_axis=2, tiled=True)
    wanted = slot_order(table_tower, table_owner, tower_id, per_tower, slot_most)
    tables = jnp.concatenate(
        [lax.dynamic_slice_in_dim(received[0], wanted[k], 1, axis=1) for k in range(per_tower)], axis=1
    )
    sample_count = tables.shape[0]
    base = tables.reshape(sample_count, feature_count)
    state = base
    for section_index in range(cross_down.shape[1]):
        current = state
        lowered = jnp.dot(
            current,
            lax.all_gather(cross_down[0, section_index], "shard", axis=0, tiled=True),
            preferred_element_type=jnp.float32,
        ).astype(jnp.bfloat16)
        raised = jnp.dot(
            lowered,
            lax.all_gather(cross_up[0, section_index], "shard", axis=1, tiled=True),
            preferred_element_type=jnp.float32,
        )
        state = (
            base.astype(jnp.float32) * (raised + cross_bias[0, section_index].astype(jnp.float32))
            + state.astype(jnp.float32)
        ).astype(jnp.bfloat16)
    squeezed = jnp.dot(
        state,
        lax.all_gather(comp_weight[0], "shard", axis=0, tiled=True),
        preferred_element_type=jnp.float32,
    )
    squeezed = (squeezed + comp_bias[0].astype(jnp.float32)).astype(jnp.bfloat16)
    tower_rows = lax.all_gather(over_weight, "shard", axis=1, tiled=True)
    summed = lax.psum_scatter(
        jnp.dot(squeezed, tower_rows, preferred_element_type=jnp.float32).astype(jnp.bfloat16),
        "tower",
        scatter_dimension=0,
        tiled=True,
    ).astype(jnp.float32)
    result = jax.nn.relu(summed + over_bias.astype(jnp.float32)).astype(jnp.bfloat16)
    return result.reshape(1, result.shape[0], result.shape[1])


def make_kernel(n, layers, tables_each, slot_most, n_devices):
    weights = 2 * layers + 1

    def kernel(
        wanted, pooled, down, up, comp, over, bias_in, over_bias, out,
        down_all, up_all, comp_all, over_all, cross_hop, comp_hop, pool_hop, received, base, state, total, lowered,
        squeezed, joined, bias, bias_wide,
        hop_send, hop_recv, first_send, first_recv, second_send, second_recv, core_send, core_recv,
        over_send, over_recv, pool_hop_send, pool_hop_recv, pool_send, pool_recv, mix_send, mix_recv, bias_send, bias_recv,
    ):
        t = lax.axis_index("tower")
        shard = lax.axis_index("shard")
        z, c = shard // CORES, shard % CORES
        other = 1 - c
        partner = (t, z * CORES + other)
        n_shard = n * CORES

        def remote(src, dst, send, recv, device):
            return pltpu.make_async_remote_copy(
                src_ref=src, dst_ref=dst, send_sem=send, recv_sem=recv,
                device_id=device, device_id_type=MESH,
            )

        barrier = pltpu.get_barrier_semaphore()
        mine = t * n_shard + shard

        @pl.loop(0, n_devices)
        def _(index):
            @pl.when(index != mine)
            def _():
                pl.semaphore_signal(
                    barrier, inc=1, device_id=(index // n_shard, index % n_shard), device_id_type=MESH
                )

        pl.semaphore_wait(barrier, n_devices - 1)

        pairs = []
        for layer in range(layers):
            pairs.append((down.at[layer], down_all.at[layer]))
            pairs.append((up.at[layer], up_all.at[layer]))
        pairs.append((comp, comp_all))

        def part(i, core, q):
            return over_all.at[q, :, core] if i == weights else pairs[i][1].at[:, core, q]

        def turn(k):
            return lax.rem(t + k, n)

        @pl.when(t == z)
        def _():
            local = pltpu.make_async_copy(bias_in, bias, bias_recv.at[0])
            local.start()
            for k in range(1, n):
                remote(bias_in, bias, bias_send.at[k], bias_recv.at[0], (turn(k), shard)).start()
            local.wait()

        def hop_of(i):
            return comp_hop if i == weights - 1 else cross_hop.at[i]

        def hop_copy(i, k):
            q = turn(k)
            return remote(
                pairs[i][0].at[q], hop_of(i).at[t], hop_send.at[i, k], hop_recv.at[i, t], (q, shard)
            )

        def hop_wait(i, k):
            tower = turn(k)
            view = hop_of(i).at[tower]
            remote(view, view, hop_send.at[i, k], hop_recv.at[i, tower], (t, shard)).wait_recv()

        def first_source(i, k):
            return pairs[i][0].at[t] if k == 0 else hop_of(i).at[turn(k)]

        def first_copy(i, k):
            return remote(
                first_source(i, k), pairs[i][1].at[z, c, t], first_send.at[i, k], first_recv.at[i, z],
                (t, turn(k) * CORES + c),
            )

        def first_local(i, k):
            return pltpu.make_async_copy(first_source(i, k), pairs[i][1].at[z, c, t], first_recv.at[i, z])

        def first_start(i, k):
            here = turn(k) == z

            @pl.when(here)
            def _():
                first_local(i, k).start()

            @pl.when(jnp.logical_not(here))
            def _():
                first_copy(i, k).start()

        def first_wait(i):
            first_local(i, 0).wait()
            for k in range(1, n):
                source = lax.rem(z + k, n)
                view = pairs[i][1].at[source, c, t]
                remote(view, view, first_send.at[i, 0], first_recv.at[i, source], (t, shard)).wait_recv()

        def over_copy(k):
            there = lax.rem(z + k, n)
            return remote(
                over, over_all.at[t, z, c], over_send.at[k], over_recv.at[z], (t, there * CORES + c)
            )

        over_local = pltpu.make_async_copy(over, over_all.at[t, z, c], over_recv.at[z])

        def over_wait():
            over_local.wait()
            for k in range(1, n):
                source = lax.rem(z + k, n)
                view = over_all.at[t, source, c]
                remote(view, view, over_send.at[k], over_recv.at[source], (t, shard)).wait_recv()

        per = slot_most // CHUNKS

        def pool_hop_copy(h, k):
            q = turn(k)
            slots = pl.ds(h * per, per)
            return remote(
                pooled.at[slots, :, :, q], pool_hop.at[t, slots], pool_hop_send.at[h, k],
                pool_hop_recv.at[h, t], (q, shard),
            )

        def pool_hop_wait(h, k):
            tower = turn(k)
            view = pool_hop.at[tower, pl.ds(h * per, per)]
            remote(view, view, pool_hop_send.at[h, k], pool_hop_recv.at[h, tower], (t, shard)).wait_recv()

        def pool_source(h, k, core):
            slots = pl.ds(h * per, per)
            return pooled.at[slots, :, core, t] if k == 0 else pool_hop.at[turn(k), slots, :, core]

        def pool_copy(h, k, core):
            return remote(
                pool_source(h, k, core), received.at[shard, pl.ds(h * per, per)],
                pool_send.at[h, k, core], pool_recv.at[h, shard], (t, turn(k) * CORES + core),
            )

        def pool_local(h, k):
            return pltpu.make_async_copy(
                pool_source(h, k, c), received.at[shard, pl.ds(h * per, per)], pool_recv.at[h, shard]
            )

        def pool_start(h, k):
            for core in range(CORES):
                here = jnp.logical_and(turn(k) == z, c == core)

                @pl.when(here)
                def _():
                    pool_local(h, k).start()

                @pl.when(jnp.logical_not(here))
                def _():
                    pool_copy(h, k, core).start()

        def pool_wait(h):
            pool_local(h, 0).wait()
            for k in range(1, n_shard):
                source = lax.rem(shard + k, n_shard)
                view = received.at[source, pl.ds(h * per, per)]
                remote(view, view, pool_send.at[h, 0, 0], pool_recv.at[h, source], (t, shard)).wait_recv()

        across, along = t % SIDE, t // SIDE
        x_next = along * SIDE + (1 - across)
        y_next = (1 - along) * SIDE + across
        diagonal = (1 - along) * SIDE + (1 - across)
        near = (t, x_next, y_next, diagonal)
        half = n // 2
        halves = (pl.ds(0, half), pl.ds(half, half))

        def second_copy(i, k):
            if k < 2:
                view = part(i, c, t)
                target = near[1 + k]
            else:
                view = part(i, c, near[k - 1]).at[halves[k - 2]]
                target = near[4 - k]
            return remote(view, view, second_send.at[i, k], second_recv.at[i, k], (target, shard))

        def second_wait(i, k):
            view = part(i, c, near[1 + k]) if k < 2 else part(i, c, diagonal).at[halves[k - 2]]
            remote(view, view, second_send.at[i, k], second_recv.at[i, k], (t, shard)).wait_recv()

        def core_copy(i, k):
            view = part(i, c, near[k])
            return remote(view, view, core_send.at[i, k], core_recv.at[i, k], partner)

        def second_start(i):
            second_copy(i, 0).start()
            second_copy(i, 1).start()
            core_copy(i, 0).start()

        def relay(i):
            for k in range(2):
                second_wait(i, k)
                second_copy(i, 2 + k).start()
                core_copy(i, 1 + k).start()

        def last(i):
            second_wait(i, 2)
            second_wait(i, 3)
            core_copy(i, 3).start()

        def complete(i):
            for k in range(n):
                view = part(i, other, near[k])
                remote(view, view, core_send.at[i, k], core_recv.at[i, k], partner).wait_recv()

        def hop_start(i):
            for k in range(1, n):
                hop_copy(i, k).start()

        def pool_hop_start(h):
            for k in range(1, n):
                pool_hop_copy(h, k).start()

        def hop_on(i):
            for k in range(1, n):
                hop_wait(i, k)
                first_start(i, k)

        def pool_on(h):
            for k in range(1, n):
                pool_hop_wait(h, k)
                pool_start(h, k)

        def spread(i):
            first_wait(i)
            second_start(i)

        ahead = 3
        for i in range(weights):
            hop_start(i)
        pool_hop_start(0)
        for i in range(ahead):
            first_start(i, 0)
        for i in range(ahead):
            hop_on(i)
        spread(0)
        pool_hop_start(1)
        for i in range(ahead, weights):
            first_start(i, 0)
            hop_on(i)
        over_local.start()
        for k in range(1, n):
            over_copy(k).start()
        for h in range(CHUNKS):
            pool_start(h, 0)
        spread(1)
        pool_hop_start(2)
        pool_on(0)
        spread(2)
        pool_hop_start(3)
        spread(3)
        pool_hop_start(4)
        pool_on(1)
        spread(4)
        pool_hop_start(5)
        over_wait()
        second_start(weights)
        relay(0)
        pool_on(2)
        relay(1)
        pool_on(3)
        relay(2)
        pool_on(4)
        relay(3)
        pool_on(5)
        relay(4)
        relay(weights)
        for i in range(weights):
            last(i)

        @pl.when(t != z)
        def _():
            remote(bias, bias, bias_send.at[0], bias_recv.at[0], (t, shard)).wait_recv()

        bias_wide[...] = bias[...].astype(F32)
        for h in range(CHUNKS):
            pool_wait(h)

        rows = base.shape[1]
        width = base.shape[2]
        emb = width // tables_each
        blocks = base.shape[0]

        @pl.loop(0, blocks)
        def _(s):
            for k in range(tables_each):
                slot = wanted[s * tables_each + k]
                base[s, :, k * emb:(k + 1) * emb] = received[slot // slot_most, slot % slot_most].reshape(rows, emb)

        for layer in range(layers):
            complete(2 * layer)
            current = base if layer == 0 else state
            total[...] = jnp.zeros_like(total)

            @pl.loop(0, blocks)
            def _(s):
                total[...] += jnp.dot(
                    current[s], down_all[layer, s // CORES, s % CORES].reshape(width, -1),
                    preferred_element_type=F32,
                )

            lowered[...] = total[...].astype(BF16)
            complete(2 * layer + 1)

            @pl.loop(0, blocks)
            def _(s):
                raised = jnp.dot(
                    lowered[...], up_all[layer, s // CORES, s % CORES].reshape(lowered.shape[1], width),
                    preferred_element_type=F32,
                )
                for k in range(tables_each):
                    cols = slice(k * emb, (k + 1) * emb)
                    row = bias_wide[pl.ds((layer * blocks + s) * tables_each + k, 1), :]
                    state[s, :, cols] = (
                        base[s, :, cols].astype(F32) * (raised[:, cols] + row)
                        + current[s, :, cols].astype(F32)
                    ).astype(BF16)

        last(weights)
        complete(2 * layers)
        cmp = squeezed.shape[2]
        total[:, :cmp] = jnp.zeros((rows, cmp), F32)

        @pl.loop(0, blocks)
        def _(s):
            total[:, :cmp] += jnp.dot(
                state[s], comp_all[s // CORES, s % CORES].reshape(width, cmp), preferred_element_type=F32
            )

        first_row = layers * blocks * tables_each
        for k in range(cmp // emb):
            cols = slice(k * emb, (k + 1) * emb)
            row = bias_wide[first_row + k:first_row + k + 1, :]
            squeezed[:, :, cols] = (total[:, cols] + row).astype(BF16).reshape(n, rows // n, emb)

        def mix_copy(k):
            there = lax.rem(z + k, n)
            return remote(
                squeezed.at[there], joined.at[z], mix_send.at[k], mix_recv.at[z], (t, there * CORES + c)
            )

        mix_local = pltpu.make_async_copy(squeezed.at[z], joined.at[z], mix_recv.at[z])
        for k in range(1, n):
            mix_copy(k).start()
        mix_local.start()
        complete(weights)
        mix_local.wait()
        for k in range(1, n):
            source = lax.rem(z + k, n)
            view = joined.at[source]
            remote(view, view, mix_send.at[k], mix_recv.at[source], (t, shard)).wait_recv()
        wide = over_all.shape[4]
        for s in range(n_shard):
            mixed = over_bias[:, s * wide:(s + 1) * wide].astype(F32)
            for tower in range(n):
                mixed = mixed + jnp.dot(
                    joined[tower], over_all[tower, s // CORES, s % CORES], preferred_element_type=F32
                )
            out[:, s * wide:(s + 1) * wide] = jnp.maximum(mixed, 0.0).astype(BF16)

        for k in range(1, n):
            over_copy(k).wait_send()
            for h in range(CHUNKS):
                pool_hop_copy(h, k).wait_send()
        for i in range(weights):
            for k in range(1, n):
                hop_copy(i, k).wait_send()
        for k in range(n):
            @pl.when(turn(k) != z)
            def _():
                for i in range(weights):
                    first_copy(i, k).wait_send()

            for core in range(CORES):
                @pl.when(jnp.logical_or(turn(k) != z, c != core))
                def _():
                    for h in range(CHUNKS):
                        pool_copy(h, k, core).wait_send()
        for i in range(weights + 1):
            for k in range(4):
                second_copy(i, k).wait_send()
                core_copy(i, k).wait_send()
        for k in range(1, n):
            mix_copy(k).wait_send()

        @pl.when(t == z)
        def _():
            for k in range(1, n):
                remote(bias_in, bias, bias_send.at[k], bias_recv.at[0], (turn(k), shard)).wait_send()

    return kernel


def turned(
    pooled, cross_down, cross_up, cross_bias, comp_weight, comp_bias, over_weight, over_bias,
    table_tower, table_owner,
):
    n = lax.axis_size("tower")
    n_shard = lax.axis_size("shard")
    layer_id = lax.axis_index("shard") // CORES
    _, samples, slot_most, emb = pooled.shape
    layers, depth, rank = cross_down.shape[1:]
    width = cross_up.shape[3]
    cmp = comp_weight.shape[2]
    tables_each = width // emb
    per_tower = tables_each * n_shard
    block = samples // (n_shard * n)
    rows = n * block
    out_width = over_bias.shape[0]
    wanted = slot_order(table_tower, table_owner, layer_id, per_tower, slot_most)
    pool_view = jnp.transpose(pooled[0], (1, 0, 2)).reshape(slot_most, n, CORES, n, block, emb)
    down = cross_down[0].reshape(layers, n, depth // n, rank)
    up = cross_up[0].reshape(layers, n, rank // n, width)
    comp = comp_weight[0].reshape(n, depth // n, cmp)
    bias_rows = jnp.concatenate([cross_bias[0].reshape(-1, emb), comp_bias[0].reshape(-1, emb)], axis=0)
    bias_rows = jnp.pad(bias_rows, ((0, -bias_rows.shape[0] % 16), (0, 0)))
    weights = 2 * layers + 1
    dma = pltpu.SemaphoreType.DMA
    any_spec = pl.BlockSpec(memory_space=pl.ANY)
    vmem_spec = pl.BlockSpec(memory_space=pltpu.VMEM)
    result = pl.pallas_call(
        make_kernel(n, layers, tables_each, slot_most, n * n_shard),
        out_shape=jax.ShapeDtypeStruct((block, out_width), BF16),
        in_specs=[pl.BlockSpec(memory_space=pltpu.SMEM)] + [any_spec] * 6 + [vmem_spec],
        out_specs=vmem_spec,
        scratch_shapes=[
            pltpu.VMEM((layers, n, CORES, n, depth // n, rank), BF16),
            pltpu.VMEM((layers, n, CORES, n, rank // n, width), BF16),
            pltpu.VMEM((n, CORES, n, depth // n, cmp), BF16),
            pltpu.VMEM((n, n, CORES) + over_weight.shape, BF16),
            pltpu.VMEM((2 * layers, n, depth // n, rank), BF16),
            pltpu.VMEM((n, depth // n, cmp), BF16),
            pltpu.VMEM((n, slot_most, n, CORES, block, emb), BF16),
            pltpu.VMEM((n_shard, slot_most, n, block, emb), BF16),
            pltpu.VMEM((n_shard, rows, width), BF16),
            pltpu.VMEM((n_shard, rows, width), BF16),
            pltpu.VMEM((rows, rank), F32),
            pltpu.VMEM((rows, rank), BF16),
            pltpu.VMEM((n, block, cmp), BF16),
            pltpu.VMEM((n, block, cmp), BF16),
            pltpu.VMEM(bias_rows.shape, BF16),
            pltpu.VMEM(bias_rows.shape, F32),
            dma((weights, n)), dma((weights, n)),
            dma((weights, n)), dma((weights, n)),
            dma((weights + 1, n)), dma((weights + 1, n)),
            dma((weights + 1, n)), dma((weights + 1, n)),
            dma((n,)), dma((n,)),
            dma((CHUNKS, n)), dma((CHUNKS, n)),
            dma((CHUNKS, n, CORES)), dma((CHUNKS, n_shard)),
            dma((n,)), dma((n,)),
            dma((n,)), dma((1,)),
        ],
        compiler_params=pltpu.CompilerParams(
            collective_id=0, has_side_effects=True, vmem_limit_bytes=60 * 1024 * 1024
        ),
        name="towers",
    )(wanted, pool_view, down, up, comp, over_weight, bias_rows, over_bias.reshape(1, -1))
    return result.reshape(1, block, out_width)


def solution(mesh):
    placed = (
        P("tower", None, "shard", None),
        P("tower", None, "shard", None),
        P("tower", None, None, "shard"),
        P("tower", None, None),
        P("tower", "shard", None),
        P("tower", None),
        P("tower", "shard"),
        P(),
        P(),
        P(),
    )
    towers, shards = mesh.shape["tower"], mesh.shape["shard"]
    body = turned if towers == SIDE * SIDE and towers * CORES == shards else on_device
    return jax.shard_map(
        body, mesh=mesh, in_specs=placed, out_specs=P("shard", "tower", None), check_vma=False
    )
```

```python
import jax
import jax.numpy as jnp
from jax import lax
from jax.experimental import pallas as pl
from jax.experimental.pallas import tpu as pltpu
from jax.sharding import PartitionSpec as P

MESH = pl.DeviceIdType.MESH
CORES = 2
SIDE = 2
BF16, F32 = jnp.bfloat16, jnp.float32


def slot_order(table_tower, table_owner, tower_id, per_tower, slot_most):
    table_count = table_tower.shape[0]
    index = jnp.arange(table_count, dtype=jnp.int32)
    inside = table_tower == tower_id
    earlier = index[None, :] < index[:, None]
    before = inside[None, :] & earlier
    position_in = jnp.sum(before.astype(jnp.int32), axis=1)
    same_owner = table_owner[None, :] == table_owner[:, None]
    own_slot = jnp.sum((before & same_owner).astype(jnp.int32), axis=1)
    wanted = table_owner * slot_most + own_slot
    picked = inside[None, :] & (
        position_in[None, :] == jnp.arange(per_tower, dtype=jnp.int32)[:, None]
    )
    return jnp.sum(jnp.where(picked, wanted[None, :], 0), axis=1)


def on_device(
    pooled,
    cross_down,
    cross_up,
    cross_bias,
    comp_weight,
    comp_bias,
    over_weight,
    over_bias,
    table_tower,
    table_owner,
):
    tower_id = lax.axis_index("tower")
    slot_most = pooled.shape[2]
    emb_width = pooled.shape[3]
    feature_count = cross_up.shape[3] * lax.axis_size("shard")
    per_tower = feature_count // emb_width
    received = lax.all_to_all(pooled, "shard", split_axis=1, concat_axis=2, tiled=True)
    wanted = slot_order(table_tower, table_owner, tower_id, per_tower, slot_most)
    tables = jnp.concatenate(
        [lax.dynamic_slice_in_dim(received[0], wanted[k], 1, axis=1) for k in range(per_tower)], axis=1
    )
    sample_count = tables.shape[0]
    base = tables.reshape(sample_count, feature_count)
    state = base
    for section_index in range(cross_down.shape[1]):
        current = state
        lowered = jnp.dot(
            current,
            lax.all_gather(cross_down[0, section_index], "shard", axis=0, tiled=True),
            preferred_element_type=jnp.float32,
        ).astype(jnp.bfloat16)
        raised = jnp.dot(
            lowered,
            lax.all_gather(cross_up[0, section_index], "shard", axis=1, tiled=True),
            preferred_element_type=jnp.float32,
        )
        state = (
            base.astype(jnp.float32) * (raised + cross_bias[0, section_index].astype(jnp.float32))
            + state.astype(jnp.float32)
        ).astype(jnp.bfloat16)
    squeezed = jnp.dot(
        state,
        lax.all_gather(comp_weight[0], "shard", axis=0, tiled=True),
        preferred_element_type=jnp.float32,
    )
    squeezed = (squeezed + comp_bias[0].astype(jnp.float32)).astype(jnp.bfloat16)
    tower_rows = lax.all_gather(over_weight, "shard", axis=1, tiled=True)
    summed = lax.psum_scatter(
        jnp.dot(squeezed, tower_rows, preferred_element_type=jnp.float32).astype(jnp.bfloat16),
        "tower",
        scatter_dimension=0,
        tiled=True,
    ).astype(jnp.float32)
    result = jax.nn.relu(summed + over_bias.astype(jnp.float32)).astype(jnp.bfloat16)
    return result.reshape(1, result.shape[0], result.shape[1])


def make_kernel(n, layers, tables_each, slot_most):
    weights = 2 * layers + 1

    def kernel(
        wanted, pooled, down, up, comp, over, bias_in, over_bias, out,
        down_all, up_all, comp_all, over_all, cross_hop, comp_hop, pool_hop, received, received_last, base, state, total, lowered,
        squeezed, joined, bias, bias_wide,
        hop_send, hop_recv, first_send, first_recv, second_send, second_recv, core_send, core_recv,
        over_send, over_recv, pool_hop_send, pool_hop_recv, pool_send, pool_recv, mix_send, mix_recv, bias_send, bias_recv,
    ):
        t = lax.axis_index("tower")
        shard = lax.axis_index("shard")
        z, c = shard // CORES, shard % CORES
        other = 1 - c
        partner = (t, z * CORES + other)
        n_shard = n * CORES

        def remote(src, dst, send, recv, device):
            return pltpu.make_async_remote_copy(
                src_ref=src, dst_ref=dst, send_sem=send, recv_sem=recv,
                device_id=device, device_id_type=MESH,
            )

        barrier = pltpu.get_barrier_semaphore()
        for k in range(1, n):
            pl.semaphore_signal(barrier, inc=1, device_id=(lax.rem(t + k, n), shard), device_id_type=MESH)
        for k in range(1, n_shard):
            pl.semaphore_signal(barrier, inc=1, device_id=(t, lax.rem(shard + k, n_shard)), device_id_type=MESH)
        pl.semaphore_wait(barrier, n + n_shard - 2)

        pairs = []
        for layer in range(layers):
            pairs.append((down.at[layer], down_all.at[layer]))
            pairs.append((up.at[layer], up_all.at[layer]))
        pairs.append((comp, comp_all))

        def part(i, core, q):
            return over_all.at[q, :, core] if i == weights else pairs[i][1].at[:, core, q]

        def turn(k):
            return lax.rem(t + k, n)

        @pl.when(t == z)
        def _():
            local = pltpu.make_async_copy(bias_in, bias, bias_recv.at[0])
            local.start()
            for k in range(1, n):
                remote(bias_in, bias, bias_send.at[k], bias_recv.at[0], (turn(k), shard)).start()
            local.wait()

        def hop_of(i):
            return comp_hop if i == weights - 1 else cross_hop.at[i]

        def hop_copy(i, k):
            q = turn(k)
            return remote(
                pairs[i][0].at[q], hop_of(i).at[t], hop_send.at[i, k], hop_recv.at[i, t], (q, shard)
            )

        def hop_wait(i, k):
            tower = turn(k)
            view = hop_of(i).at[tower]
            remote(view, view, hop_send.at[i, k], hop_recv.at[i, tower], (t, shard)).wait_recv()

        def first_source(i, k):
            return pairs[i][0].at[t] if k == 0 else hop_of(i).at[turn(k)]

        def first_copy(i, k):
            return remote(
                first_source(i, k), pairs[i][1].at[z, c, t], first_send.at[i, k], first_recv.at[i, z],
                (t, turn(k) * CORES + c),
            )

        def first_local(i, k):
            return pltpu.make_async_copy(first_source(i, k), pairs[i][1].at[z, c, t], first_recv.at[i, z])

        def first_start(i, k):
            here = turn(k) == z

            @pl.when(here)
            def _():
                first_local(i, k).start()

            @pl.when(jnp.logical_not(here))
            def _():
                first_copy(i, k).start()

        def first_wait(i):
            first_local(i, 0).wait()
            for k in range(1, n):
                source = lax.rem(z + k, n)
                view = pairs[i][1].at[source, c, t]
                remote(view, view, first_send.at[i, 0], first_recv.at[i, source], (t, shard)).wait_recv()

        def over_copy(k):
            there = lax.rem(z + k, n)
            return remote(
                over, over_all.at[t, z, c], over_send.at[k], over_recv.at[z], (t, there * CORES + c)
            )

        over_local = pltpu.make_async_copy(over, over_all.at[t, z, c], over_recv.at[z])

        def over_wait():
            over_local.wait()
            for k in range(1, n):
                source = lax.rem(z + k, n)
                view = over_all.at[t, source, c]
                remote(view, view, over_send.at[k], over_recv.at[source], (t, shard)).wait_recv()

        def pool_hop_copy(h, k):
            q = turn(k)
            return remote(
                pooled.at[:, h, :, q], pool_hop.at[t, :, h], pool_hop_send.at[h, k], pool_hop_recv.at[h, t], (q, shard)
            )

        def pool_hop_wait(h, k):
            tower = turn(k)
            view = pool_hop.at[tower, :, h]
            remote(view, view, pool_hop_send.at[h, k], pool_hop_recv.at[h, tower], (t, shard)).wait_recv()

        def pool_source(h, k, core):
            return pooled.at[:, h, core, t] if k == 0 else pool_hop.at[turn(k), :, h, core]

        def pool_place(h, owner):
            return received.at[owner, :, h] if h < n - 1 else received_last.at[owner]

        def pool_copy(h, k, core):
            return remote(
                pool_source(h, k, core), pool_place(h, shard), pool_send.at[h, k, core], pool_recv.at[h, shard],
                (t, turn(k) * CORES + core),
            )

        def pool_local(h, k):
            return pltpu.make_async_copy(pool_source(h, k, c), pool_place(h, shard), pool_recv.at[h, shard])

        def pool_start(h, k):
            for core in range(CORES):
                here = jnp.logical_and(turn(k) == z, c == core)

                @pl.when(here)
                def _():
                    pool_local(h, k).start()

                @pl.when(jnp.logical_not(here))
                def _():
                    pool_copy(h, k, core).start()

        def pool_wait(h):
            pool_local(h, 0).wait()
            for k in range(1, n_shard):
                source = lax.rem(shard + k, n_shard)
                view = pool_place(h, source)
                remote(view, view, pool_send.at[h, 0, 0], pool_recv.at[h, source], (t, shard)).wait_recv()

        across, along = t % SIDE, t // SIDE
        x_next = along * SIDE + (1 - across)
        y_next = (1 - along) * SIDE + across
        diagonal = (1 - along) * SIDE + (1 - across)
        near = (t, x_next, y_next, diagonal)
        half = n // 2
        halves = (pl.ds(0, half), pl.ds(half, half))

        def second_copy(i, k):
            if k < 2:
                view = part(i, c, t)
                target = near[1 + k]
            else:
                view = part(i, c, near[k - 1]).at[halves[k - 2]]
                target = near[4 - k]
            return remote(view, view, second_send.at[i, k], second_recv.at[i, k], (target, shard))

        def second_wait(i, k):
            view = part(i, c, near[1 + k]) if k < 2 else part(i, c, diagonal).at[halves[k - 2]]
            remote(view, view, second_send.at[i, k], second_recv.at[i, k], (t, shard)).wait_recv()

        def core_copy(i, k):
            view = part(i, c, near[k])
            return remote(view, view, core_send.at[i, k], core_recv.at[i, k], partner)

        def second_start(i):
            second_copy(i, 0).start()
            second_copy(i, 1).start()
            core_copy(i, 0).start()

        def relay(i):
            for k in range(2):
                second_wait(i, k)
                second_copy(i, 2 + k).start()
                core_copy(i, 1 + k).start()

        def last(i):
            second_wait(i, 2)
            second_wait(i, 3)
            core_copy(i, 3).start()

        def complete(i):
            for k in range(n):
                view = part(i, other, near[k])
                remote(view, view, core_send.at[i, k], core_recv.at[i, k], partner).wait_recv()

        def hop_start(i):
            for k in range(1, n):
                hop_copy(i, k).start()

        def pool_hop_start(h):
            for k in range(1, n):
                pool_hop_copy(h, k).start()

        def hop_on(i):
            for k in range(1, n):
                hop_wait(i, k)
                first_start(i, k)

        def pool_on(h):
            for k in range(1, n):
                pool_hop_wait(h, k)
                pool_start(h, k)

        def spread(i):
            first_wait(i)
            second_start(i)

        rows = base.shape[1]
        width = base.shape[2]
        emb = width // tables_each
        blocks = base.shape[0]
        block = rows // n
        cmp = squeezed.shape[2]

        def gather(source, lo, hi):
            @pl.loop(0, blocks)
            def _(s):
                for k in range(tables_each):
                    slot = wanted[s * tables_each + k]
                    base[s, lo:hi, k * emb:(k + 1) * emb] = source[slot // slot_most, slot % slot_most].reshape(
                        hi - lo, emb
                    )

        def lower(layer, lo, hi):
            current = base if layer == 0 else state
            total[lo:hi, :] = jnp.zeros((hi - lo, total.shape[1]), F32)

            @pl.loop(0, blocks)
            def _(s):
                total[lo:hi, :] += jnp.dot(
                    current[s, lo:hi, :], down_all[layer, s // CORES, s % CORES].reshape(width, -1),
                    preferred_element_type=F32,
                )

            lowered[lo:hi, :] = total[lo:hi, :].astype(BF16)

        def cross(layer, lo, hi):
            current = base if layer == 0 else state

            @pl.loop(0, blocks)
            def _(s):
                raised = jnp.dot(
                    lowered[lo:hi, :], up_all[layer, s // CORES, s % CORES].reshape(lowered.shape[1], width),
                    preferred_element_type=F32,
                )
                for k in range(tables_each):
                    cols = slice(k * emb, (k + 1) * emb)
                    row = bias_wide[pl.ds((layer * blocks + s) * tables_each + k, 1), :]
                    state[s, lo:hi, cols] = (
                        base[s, lo:hi, cols].astype(F32) * (raised[:, cols] + row)
                        + current[s, lo:hi, cols].astype(F32)
                    ).astype(BF16)

        def mix_copy(there):
            return remote(
                squeezed.at[there], joined.at[z], mix_send.at[there], mix_recv.at[z], (t, there * CORES + c)
            )

        mix_local = pltpu.make_async_copy(squeezed.at[z], joined.at[z], mix_recv.at[z])

        def squeeze(lo, hi):
            total[lo:hi, :cmp] = jnp.zeros((hi - lo, cmp), F32)

            @pl.loop(0, blocks)
            def _(s):
                total[lo:hi, :cmp] += jnp.dot(
                    state[s, lo:hi, :], comp_all[s // CORES, s % CORES].reshape(width, cmp), preferred_element_type=F32
                )

            first_row = layers * blocks * tables_each
            for k in range(cmp // emb):
                cols = slice(k * emb, (k + 1) * emb)
                row = bias_wide[first_row + k:first_row + k + 1, :]
                squeezed[lo // block:hi // block, :, cols] = (
                    (total[lo:hi, cols] + row).astype(BF16).reshape((hi - lo) // block, block, emb)
                )
            for there in range(lo // block, hi // block):
                @pl.when(z == there)
                def _():
                    mix_local.start()

                @pl.when(z != there)
                def _():
                    mix_copy(there).start()

        comp_id, over_id = weights - 1, weights
        hop_start(comp_id)
        for i in range(comp_id):
            hop_start(i)
        pool_hop_start(0)
        for i in (comp_id, 0, 1):
            first_start(i, 0)
        for i in (comp_id, 0, 1):
            hop_on(i)
        spread(comp_id)
        first_start(2, 0)
        hop_on(2)
        spread(0)
        first_start(3, 0)
        hop_on(3)
        over_local.start()
        for k in range(1, n):
            over_copy(k).start()
        for h in range(n):
            pool_start(h, 0)
        spread(1)
        pool_hop_start(1)
        pool_on(0)
        spread(2)
        pool_hop_start(2)
        spread(3)
        relay(comp_id)
        pool_on(1)
        relay(0)
        relay(1)
        pool_hop_start(3)
        pool_on(2)
        relay(2)
        relay(3)
        over_wait()
        second_start(over_id)
        pool_on(3)
        last(comp_id)
        last(0)

        @pl.when(t != z)
        def _():
            remote(bias, bias, bias_send.at[0], bias_recv.at[0], (t, shard)).wait_recv()

        bias_wide[...] = bias[...].astype(F32)
        for h in range(n - 1):
            pool_wait(h)
        early, late = (0, rows - block), (rows - block, rows)
        gather(received, *early)
        complete(0)
        lower(0, *early)
        last(1)
        complete(1)
        cross(0, *early)
        last(2)
        complete(2)
        lower(1, *early)
        relay(over_id)
        last(3)
        complete(3)
        cross(1, *early)
        complete(comp_id)
        squeeze(*early)
        last(over_id)
        pool_wait(n - 1)
        gather(received_last, *late)
        for layer in range(layers):
            lower(layer, *late)
            cross(layer, *late)
        squeeze(*late)
        complete(over_id)
        mix_local.wait()
        for k in range(1, n):
            source = lax.rem(z + k, n)
            view = joined.at[source]
            remote(view, view, mix_send.at[0], mix_recv.at[source], (t, shard)).wait_recv()
        wide = over_all.shape[4]
        for s in range(n_shard):
            mixed = over_bias[:, s * wide:(s + 1) * wide].astype(F32)
            for tower in range(n):
                mixed = mixed + jnp.dot(
                    joined[tower], over_all[tower, s // CORES, s % CORES], preferred_element_type=F32
                )
            out[:, s * wide:(s + 1) * wide] = jnp.maximum(mixed, 0.0).astype(BF16)

        for k in range(1, n):
            over_copy(k).wait_send()
            for h in range(n):
                pool_hop_copy(h, k).wait_send()
        for i in range(weights):
            for k in range(1, n):
                hop_copy(i, k).wait_send()
        for k in range(n):
            @pl.when(turn(k) != z)
            def _():
                for i in range(weights):
                    first_copy(i, k).wait_send()

            for core in range(CORES):
                @pl.when(jnp.logical_or(turn(k) != z, c != core))
                def _():
                    for h in range(n):
                        pool_copy(h, k, core).wait_send()
        for i in range(weights + 1):
            for k in range(4):
                second_copy(i, k).wait_send()
                core_copy(i, k).wait_send()
        for there in range(n):
            @pl.when(z != there)
            def _():
                mix_copy(there).wait_send()

        @pl.when(t == z)
        def _():
            for k in range(1, n):
                remote(bias_in, bias, bias_send.at[k], bias_recv.at[0], (turn(k), shard)).wait_send()

    return kernel


def turned(
    pooled, cross_down, cross_up, cross_bias, comp_weight, comp_bias, over_weight, over_bias,
    table_tower, table_owner,
):
    n = lax.axis_size("tower")
    n_shard = lax.axis_size("shard")
    layer_id = lax.axis_index("shard") // CORES
    _, samples, slot_most, emb = pooled.shape
    layers, depth, rank = cross_down.shape[1:]
    width = cross_up.shape[3]
    cmp = comp_weight.shape[2]
    tables_each = width // emb
    per_tower = tables_each * n_shard
    block = samples // (n_shard * n)
    rows = n * block
    out_width = over_bias.shape[0]
    wanted = slot_order(table_tower, table_owner, layer_id, per_tower, slot_most)
    pool_view = jnp.transpose(pooled[0], (1, 0, 2)).reshape(slot_most, n, CORES, n, block, emb)
    down = cross_down[0].reshape(layers, n, depth // n, rank)
    up = cross_up[0].reshape(layers, n, rank // n, width)
    comp = comp_weight[0].reshape(n, depth // n, cmp)
    bias_rows = jnp.concatenate([cross_bias[0].reshape(-1, emb), comp_bias[0].reshape(-1, emb)], axis=0)
    bias_rows = jnp.pad(bias_rows, ((0, -bias_rows.shape[0] % 16), (0, 0)))
    weights = 2 * layers + 1
    dma = pltpu.SemaphoreType.DMA
    any_spec = pl.BlockSpec(memory_space=pl.ANY)
    vmem_spec = pl.BlockSpec(memory_space=pltpu.VMEM)
    result = pl.pallas_call(
        make_kernel(n, layers, tables_each, slot_most),
        out_shape=jax.ShapeDtypeStruct((block, out_width), BF16),
        in_specs=[pl.BlockSpec(memory_space=pltpu.SMEM)] + [any_spec] * 6 + [vmem_spec],
        out_specs=vmem_spec,
        scratch_shapes=[
            pltpu.VMEM((layers, n, CORES, n, depth // n, rank), BF16),
            pltpu.VMEM((layers, n, CORES, n, rank // n, width), BF16),
            pltpu.VMEM((n, CORES, n, depth // n, cmp), BF16),
            pltpu.VMEM((n, n, CORES) + over_weight.shape, BF16),
            pltpu.VMEM((2 * layers, n, depth // n, rank), BF16),
            pltpu.VMEM((n, depth // n, cmp), BF16),
            pltpu.VMEM((n, slot_most, n, CORES, block, emb), BF16),
            pltpu.VMEM((n_shard, slot_most, n - 1, block, emb), BF16),
            pltpu.VMEM((n_shard, slot_most, block, emb), BF16),
            pltpu.VMEM((n_shard, rows, width), BF16),
            pltpu.VMEM((n_shard, rows, width), BF16),
            pltpu.VMEM((rows, rank), F32),
            pltpu.VMEM((rows, rank), BF16),
            pltpu.VMEM((n, block, cmp), BF16),
            pltpu.VMEM((n, block, cmp), BF16),
            pltpu.VMEM(bias_rows.shape, BF16),
            pltpu.VMEM(bias_rows.shape, F32),
            dma((weights, n)), dma((weights, n)),
            dma((weights, n)), dma((weights, n)),
            dma((weights + 1, n)), dma((weights + 1, n)),
            dma((weights + 1, n)), dma((weights + 1, n)),
            dma((n,)), dma((n,)),
            dma((n, n)), dma((n, n)),
            dma((n, n, CORES)), dma((n, n_shard)),
            dma((n,)), dma((n,)),
            dma((n,)), dma((1,)),
        ],
        compiler_params=pltpu.CompilerParams(
            collective_id=0, has_side_effects=True, vmem_limit_bytes=60 * 1024 * 1024
        ),
        name="towers",
    )(wanted, pool_view, down, up, comp, over_weight, bias_rows, over_bias.reshape(1, -1))
    return result.reshape(1, block, out_width)


def solution(mesh):
    placed = (
        P("tower", None, "shard", None),
        P("tower", None, "shard", None),
        P("tower", None, None, "shard"),
        P("tower", None, None),
        P("tower", "shard", None),
        P("tower", None),
        P("tower", "shard"),
        P(),
        P(),
        P(),
    )
    towers, shards = mesh.shape["tower"], mesh.shape["shard"]
    body = turned if towers == SIDE * SIDE and towers * CORES == shards else on_device
    return jax.shard_map(
        body, mesh=mesh, in_specs=placed, out_specs=P("shard", "tower", None), check_vma=False
    )
```

```python
import jax
import jax.numpy as jnp
from jax import lax
from jax.experimental import pallas as pl
from jax.experimental.pallas import tpu as pltpu
from jax.sharding import PartitionSpec as P

MESH = pl.DeviceIdType.MESH
CORES = 2
SIDE = 2
BF16, F32 = jnp.bfloat16, jnp.float32


def slot_order(table_tower, table_owner, tower_id, per_tower, slot_most):
    table_count = table_tower.shape[0]
    index = jnp.arange(table_count, dtype=jnp.int32)
    inside = table_tower == tower_id
    earlier = index[None, :] < index[:, None]
    before = inside[None, :] & earlier
    position_in = jnp.sum(before.astype(jnp.int32), axis=1)
    same_owner = table_owner[None, :] == table_owner[:, None]
    own_slot = jnp.sum((before & same_owner).astype(jnp.int32), axis=1)
    wanted = table_owner * slot_most + own_slot
    picked = inside[None, :] & (
        position_in[None, :] == jnp.arange(per_tower, dtype=jnp.int32)[:, None]
    )
    return jnp.sum(jnp.where(picked, wanted[None, :], 0), axis=1)


def on_device(
    pooled,
    cross_down,
    cross_up,
    cross_bias,
    comp_weight,
    comp_bias,
    over_weight,
    over_bias,
    table_tower,
    table_owner,
):
    tower_id = lax.axis_index("tower")
    slot_most = pooled.shape[2]
    emb_width = pooled.shape[3]
    feature_count = cross_up.shape[3] * lax.axis_size("shard")
    per_tower = feature_count // emb_width
    received = lax.all_to_all(pooled, "shard", split_axis=1, concat_axis=2, tiled=True)
    wanted = slot_order(table_tower, table_owner, tower_id, per_tower, slot_most)
    tables = jnp.concatenate(
        [lax.dynamic_slice_in_dim(received[0], wanted[k], 1, axis=1) for k in range(per_tower)], axis=1
    )
    sample_count = tables.shape[0]
    base = tables.reshape(sample_count, feature_count)
    state = base
    for section_index in range(cross_down.shape[1]):
        current = state
        lowered = jnp.dot(
            current,
            lax.all_gather(cross_down[0, section_index], "shard", axis=0, tiled=True),
            preferred_element_type=jnp.float32,
        ).astype(jnp.bfloat16)
        raised = jnp.dot(
            lowered,
            lax.all_gather(cross_up[0, section_index], "shard", axis=1, tiled=True),
            preferred_element_type=jnp.float32,
        )
        state = (
            base.astype(jnp.float32) * (raised + cross_bias[0, section_index].astype(jnp.float32))
            + state.astype(jnp.float32)
        ).astype(jnp.bfloat16)
    squeezed = jnp.dot(
        state,
        lax.all_gather(comp_weight[0], "shard", axis=0, tiled=True),
        preferred_element_type=jnp.float32,
    )
    squeezed = (squeezed + comp_bias[0].astype(jnp.float32)).astype(jnp.bfloat16)
    tower_rows = lax.all_gather(over_weight, "shard", axis=1, tiled=True)
    summed = lax.psum_scatter(
        jnp.dot(squeezed, tower_rows, preferred_element_type=jnp.float32).astype(jnp.bfloat16),
        "tower",
        scatter_dimension=0,
        tiled=True,
    ).astype(jnp.float32)
    result = jax.nn.relu(summed + over_bias.astype(jnp.float32)).astype(jnp.bfloat16)
    return result.reshape(1, result.shape[0], result.shape[1])


def make_kernel(n, layers, tables_each, slot_most):
    weights = 2 * layers + 1

    def kernel(
        table_tower, table_owner, pooled, down, up, comp, over, cross_bias, comp_bias, over_bias, out,
        down_all, up_all, comp_all, over_all, cross_hop, comp_hop, pool_hop, received, received_last, base, state, total, lowered,
        squeezed, joined, bias, bias_low, bias_wide, order_row, wanted, order_sem,
        hop_send, hop_recv, first_send, first_recv, second_send, second_recv, core_send, core_recv,
        over_send, over_recv, pool_hop_send, pool_hop_recv, pool_send, pool_recv, mix_send, mix_recv, bias_send, bias_recv,
    ):
        t = lax.axis_index("tower")
        shard = lax.axis_index("shard")
        z, c = shard // CORES, shard % CORES
        other = 1 - c
        partner = (t, z * CORES + other)
        n_shard = n * CORES

        def remote(src, dst, send, recv, device):
            return pltpu.make_async_remote_copy(
                src_ref=src, dst_ref=dst, send_sem=send, recv_sem=recv,
                device_id=device, device_id_type=MESH,
            )

        barrier = pltpu.get_barrier_semaphore()
        for k in range(1, n):
            pl.semaphore_signal(barrier, inc=1, device_id=(lax.rem(t + k, n), shard), device_id_type=MESH)
        for k in range(1, n_shard):
            pl.semaphore_signal(barrier, inc=1, device_id=(t, lax.rem(shard + k, n_shard)), device_id_type=MESH)
        pl.semaphore_wait(barrier, n + n_shard - 2)

        pairs = []
        for layer in range(layers):
            pairs.append((down.at[layer], down_all.at[layer]))
            pairs.append((up.at[layer], up_all.at[layer]))
        pairs.append((comp, comp_all))

        def part(i, core, q):
            return over_all.at[q, :, core] if i == weights else pairs[i][1].at[:, core, q]

        def turn(k):
            return lax.rem(t + k, n)

        biases = ((cross_bias, bias), (comp_bias, bias_low))

        @pl.when(t == z)
        def _():
            for i, (source, place) in enumerate(biases):
                pltpu.make_async_copy(source, place, bias_recv.at[i]).start()
                for k in range(1, n):
                    remote(source, place, bias_send.at[i, k], bias_recv.at[i], (turn(k), shard)).start()

        def order_tables():
            count = table_tower.shape[0]
            rows_of = lax.broadcasted_iota(jnp.int32, (count, count), 0)
            cols_of = lax.broadcasted_iota(jnp.int32, (count, count), 1)

            def column(row):
                return jnp.sum(jnp.where(rows_of == cols_of, row, 0), axis=1, keepdims=True)

            owner = table_owner[...].reshape(1, count)
            inside = (table_tower[...].reshape(1, count) == z).astype(jnp.int32)
            before = jnp.where(rows_of < cols_of, column(inside), 0)
            position = jnp.sum(before, axis=0, keepdims=True)
            own_slot = jnp.sum(jnp.where(column(owner) == owner, before, 0), axis=0, keepdims=True)
            slot = owner * slot_most + own_slot
            place = jnp.where(inside == 1, position, count)
            order_row[...] = jnp.sum(
                jnp.where(column(place) == cols_of, column(slot), 0), axis=0, keepdims=True
            )
            pltpu.make_async_copy(order_row, wanted, order_sem.at[0]).start()

        def hop_of(i):
            return comp_hop if i == weights - 1 else cross_hop.at[i]

        def hop_copy(i, k):
            q = turn(k)
            return remote(
                pairs[i][0].at[q], hop_of(i).at[t], hop_send.at[i, k], hop_recv.at[i, t], (q, shard)
            )

        def hop_wait(i, k):
            tower = turn(k)
            view = hop_of(i).at[tower]
            remote(view, view, hop_send.at[i, k], hop_recv.at[i, tower], (t, shard)).wait_recv()

        def first_source(i, k):
            return pairs[i][0].at[t] if k == 0 else hop_of(i).at[turn(k)]

        def first_copy(i, k):
            return remote(
                first_source(i, k), pairs[i][1].at[z, c, t], first_send.at[i, k], first_recv.at[i, z],
                (t, turn(k) * CORES + c),
            )

        def first_local(i, k):
            return pltpu.make_async_copy(first_source(i, k), pairs[i][1].at[z, c, t], first_recv.at[i, z])

        def first_start(i, k):
            here = turn(k) == z

            @pl.when(here)
            def _():
                first_local(i, k).start()

            @pl.when(jnp.logical_not(here))
            def _():
                first_copy(i, k).start()

        def first_wait(i):
            first_local(i, 0).wait()
            for k in range(1, n):
                source = lax.rem(z + k, n)
                view = pairs[i][1].at[source, c, t]
                remote(view, view, first_send.at[i, 0], first_recv.at[i, source], (t, shard)).wait_recv()

        def over_copy(k):
            there = lax.rem(z + k, n)
            return remote(
                over, over_all.at[t, z, c], over_send.at[k], over_recv.at[z], (t, there * CORES + c)
            )

        over_local = pltpu.make_async_copy(over, over_all.at[t, z, c], over_recv.at[z])

        def over_wait():
            over_local.wait()
            for k in range(1, n):
                source = lax.rem(z + k, n)
                view = over_all.at[t, source, c]
                remote(view, view, over_send.at[k], over_recv.at[source], (t, shard)).wait_recv()

        def pool_hop_copy(h, k):
            q = turn(k)
            return remote(
                pooled.at[:, turn(1 + h), :, q], pool_hop.at[t, :, h], pool_hop_send.at[h, k], pool_hop_recv.at[h, t], (q, shard)
            )

        def pool_hop_wait(h, k):
            tower = turn(k)
            view = pool_hop.at[tower, :, h]
            remote(view, view, pool_hop_send.at[h, k], pool_hop_recv.at[h, tower], (t, shard)).wait_recv()

        def pool_source(h, k, core):
            return pooled.at[:, turn(1 + h), core, t] if k == 0 else pool_hop.at[turn(k), :, h, core]

        def pool_place(h, owner):
            return received.at[owner, :, h] if h < n - 1 else received_last.at[owner]

        def pool_copy(h, k, core):
            return remote(
                pool_source(h, k, core), pool_place(h, shard), pool_send.at[h, k, core], pool_recv.at[h, shard],
                (t, turn(k) * CORES + core),
            )

        def pool_local(h, k):
            return pltpu.make_async_copy(pool_source(h, k, c), pool_place(h, shard), pool_recv.at[h, shard])

        def pool_start(h, k):
            for core in range(CORES):
                here = jnp.logical_and(turn(k) == z, c == core)

                @pl.when(here)
                def _():
                    pool_local(h, k).start()

                @pl.when(jnp.logical_not(here))
                def _():
                    pool_copy(h, k, core).start()

        def pool_wait(h):
            pool_local(h, 0).wait()
            for k in range(1, n_shard):
                source = lax.rem(shard + k, n_shard)
                view = pool_place(h, source)
                remote(view, view, pool_send.at[h, 0, 0], pool_recv.at[h, source], (t, shard)).wait_recv()

        across, along = t % SIDE, t // SIDE
        x_next = along * SIDE + (1 - across)
        y_next = (1 - along) * SIDE + across
        diagonal = (1 - along) * SIDE + (1 - across)
        near = (t, x_next, y_next, diagonal)
        half = n // 2
        halves = (pl.ds(0, half), pl.ds(half, half))

        def second_copy(i, k):
            if k < 2:
                view = part(i, c, t)
                target = near[1 + k]
            else:
                view = part(i, c, near[k - 1]).at[halves[k - 2]]
                target = near[4 - k]
            return remote(view, view, second_send.at[i, k], second_recv.at[i, k], (target, shard))

        def second_wait(i, k):
            view = part(i, c, near[1 + k]) if k < 2 else part(i, c, diagonal).at[halves[k - 2]]
            remote(view, view, second_send.at[i, k], second_recv.at[i, k], (t, shard)).wait_recv()

        def core_copy(i, k):
            view = part(i, c, near[k])
            return remote(view, view, core_send.at[i, k], core_recv.at[i, k], partner)

        def second_start(i):
            second_copy(i, 0).start()
            second_copy(i, 1).start()
            core_copy(i, 0).start()

        def relay(i):
            for k in range(2):
                second_wait(i, k)
                second_copy(i, 2 + k).start()
                core_copy(i, 1 + k).start()

        def last(i):
            second_wait(i, 2)
            second_wait(i, 3)
            core_copy(i, 3).start()

        def complete(i):
            for k in range(n):
                view = part(i, other, near[k])
                remote(view, view, core_send.at[i, k], core_recv.at[i, k], partner).wait_recv()

        def hop_start(i):
            for k in range(1, n):
                hop_copy(i, k).start()

        def pool_hop_start(h):
            for k in range(1, n):
                pool_hop_copy(h, k).start()

        def hop_on(i):
            for k in range(1, n):
                hop_wait(i, k)
                first_start(i, k)

        def pool_on(h):
            for k in range(1, n):
                pool_hop_wait(h, k)
                pool_start(h, k)

        def spread(i):
            first_wait(i)
            second_start(i)

        rows = base.shape[1]
        width = base.shape[2]
        emb = width // tables_each
        blocks = base.shape[0]
        block = rows // n
        cmp = squeezed.shape[2]

        def gather(source, lo, hi):
            @pl.loop(0, blocks, unroll=True)
            def _(s):
                for k in range(tables_each):
                    slot = wanted[0, s * tables_each + k]
                    base[s, lo:hi, k * emb:(k + 1) * emb] = source[slot // slot_most, slot % slot_most].reshape(
                        hi - lo, emb
                    )

        def lower(layer, lo, hi):
            current = base if layer == 0 else state
            if hi - lo > rows:
                total[lo:hi, :] = jnp.zeros((hi - lo, total.shape[1]), F32)

                @pl.loop(0, blocks)
                def _(s):
                    total[lo:hi, :] += jnp.dot(
                        current[s, lo:hi, :], down_all[layer, s // CORES, s % CORES].reshape(width, -1),
                        preferred_element_type=F32,
                    )

                lowered[lo:hi, :] = total[lo:hi, :].astype(BF16)
            else:
                added = jnp.zeros((hi - lo, total.shape[1]), F32)
                for s in range(blocks):
                    added = added + jnp.dot(
                        current[s, lo:hi, :], down_all[layer, s // CORES, s % CORES].reshape(width, -1),
                        preferred_element_type=F32,
                    )
                lowered[lo:hi, :] = added.astype(BF16)

        def cross(layer, lo, hi):
            current = base if layer == 0 else state

            @pl.loop(0, blocks, unroll=True)
            def _(s):
                raised = jnp.dot(
                    lowered[lo:hi, :], up_all[layer, s // CORES, s % CORES].reshape(lowered.shape[1], width),
                    preferred_element_type=F32,
                )
                for k in range(tables_each):
                    cols = slice(k * emb, (k + 1) * emb)
                    row = bias_wide[layer:layer + 1, pl.ds(pl.multiple_of((s * tables_each + k) * emb, emb), emb)]
                    state[s, lo:hi, cols] = (
                        base[s, lo:hi, cols].astype(F32) * (raised[:, cols] + row)
                        + current[s, lo:hi, cols].astype(F32)
                    ).astype(BF16)

        def mix_copy(h):
            there = lax.rem(z + 1 + h, n)
            return remote(squeezed.at[h], joined.at[z], mix_send.at[h], mix_recv.at[z], (t, there * CORES + c))

        def squeeze(lo, hi):
            added = jnp.zeros((hi - lo, cmp), F32)
            for s in range(blocks):
                added = added + jnp.dot(
                    state[s, lo:hi, :], comp_all[s // CORES, s % CORES].reshape(width, cmp), preferred_element_type=F32
                )
            for k in range(cmp // emb):
                cols = slice(k * emb, (k + 1) * emb)
                row = bias_low[:, cols].astype(F32)
                squeezed[lo // block:hi // block, :, cols] = (
                    (added[:, cols] + row).astype(BF16).reshape((hi - lo) // block, block, emb)
                )

        comp_id, over_id = weights - 1, weights
        hop_start(comp_id)
        for i in range(comp_id):
            hop_start(i)
        pool_hop_start(0)
        for i in (comp_id, 0, 1):
            first_start(i, 0)
        order_tables()
        for i in (comp_id, 0, 1):
            hop_on(i)
        spread(comp_id)
        first_start(2, 0)
        hop_on(2)
        spread(0)
        first_start(3, 0)
        hop_on(3)
        over_local.start()
        for k in range(1, n):
            over_copy(k).start()
        for h in range(n):
            pool_start(h, 0)
        spread(1)
        pool_hop_start(1)
        pool_on(0)
        spread(2)
        pool_hop_start(2)
        spread(3)
        relay(comp_id)
        pool_on(1)
        relay(0)
        relay(1)
        pool_hop_start(3)
        pool_on(2)
        relay(2)
        relay(3)
        over_wait()
        second_start(over_id)
        pool_on(3)
        last(comp_id)
        last(0)

        for i, (source, place) in enumerate(biases):
            @pl.when(t == z)
            def _():
                pltpu.make_async_copy(source, place, bias_recv.at[i]).wait()

            @pl.when(t != z)
            def _():
                remote(place, place, bias_send.at[i, 0], bias_recv.at[i], (t, shard)).wait_recv()

        bias_wide[...] = bias[...].astype(F32)
        pltpu.make_async_copy(order_row, wanted, order_sem.at[0]).wait()
        for h in range(n - 1):
            pool_wait(h)
        early, late = (0, rows - block), (rows - block, rows)
        gather(received, *early)
        complete(0)
        lower(0, *early)
        last(1)
        complete(1)
        cross(0, *early)
        last(2)
        complete(2)
        lower(1, *early)
        relay(over_id)
        last(3)
        complete(3)
        cross(1, *early)
        complete(comp_id)
        squeeze(*early)
        for h in range(n - 1):
            mix_copy(h).start()
        last(over_id)
        pool_wait(n - 1)
        gather(received_last, *late)
        for layer in range(layers):
            lower(layer, *late)
            cross(layer, *late)
        squeeze(*late)
        complete(over_id)
        for k in range(1, n):
            source = lax.rem(z + k, n)
            view = joined.at[source]
            remote(view, view, mix_send.at[0], mix_recv.at[source], (t, shard)).wait_recv()
        wide = over_all.shape[4]
        for s in range(n_shard):
            mixed = over_bias[s * wide:(s + 1) * wide].astype(F32).reshape(1, wide)
            for k in range(n):
                tower = lax.rem(z + k, n)
                part_in = squeezed[n - 1] if k == 0 else joined[tower]
                mixed = mixed + jnp.dot(
                    part_in, over_all[tower, s // CORES, s % CORES], preferred_element_type=F32
                )
            out[:, s * wide:(s + 1) * wide] = jnp.maximum(mixed, 0.0).astype(BF16)

        for k in range(1, n):
            over_copy(k).wait_send()
            for h in range(n):
                pool_hop_copy(h, k).wait_send()
        for i in range(weights):
            for k in range(1, n):
                hop_copy(i, k).wait_send()
        for k in range(n):
            @pl.when(turn(k) != z)
            def _():
                for i in range(weights):
                    first_copy(i, k).wait_send()

            for core in range(CORES):
                @pl.when(jnp.logical_or(turn(k) != z, c != core))
                def _():
                    for h in range(n):
                        pool_copy(h, k, core).wait_send()
        for i in range(weights + 1):
            for k in range(4):
                second_copy(i, k).wait_send()
                core_copy(i, k).wait_send()
        for h in range(n - 1):
            mix_copy(h).wait_send()

        @pl.when(t == z)
        def _():
            for i, (source, place) in enumerate(biases):
                for k in range(1, n):
                    remote(source, place, bias_send.at[i, k], bias_recv.at[i], (turn(k), shard)).wait_send()

    return kernel


def turned(
    pooled, cross_down, cross_up, cross_bias, comp_weight, comp_bias, over_weight, over_bias,
    table_tower, table_owner,
):
    n = lax.axis_size("tower")
    n_shard = lax.axis_size("shard")
    _, samples, slot_most, emb = pooled.shape
    layers, depth, rank = cross_down.shape[1:]
    width = cross_up.shape[3]
    cmp = comp_weight.shape[2]
    tables_each = width // emb
    block = samples // (n_shard * n)
    rows = n * block
    out_width = over_bias.shape[0]
    pool_view = jnp.transpose(pooled[0], (1, 0, 2)).reshape(slot_most, n, CORES, n, block, emb)
    down = cross_down[0].reshape(layers, n, depth // n, rank)
    up = cross_up[0].reshape(layers, n, rank // n, width)
    comp = comp_weight[0].reshape(n, depth // n, cmp)
    weights = 2 * layers + 1
    dma = pltpu.SemaphoreType.DMA
    any_spec = pl.BlockSpec(memory_space=pl.ANY)
    vmem_spec = pl.BlockSpec(memory_space=pltpu.VMEM)
    result = pl.pallas_call(
        make_kernel(n, layers, tables_each, slot_most),
        out_shape=jax.ShapeDtypeStruct((block, out_width), BF16),
        in_specs=[vmem_spec] * 2 + [any_spec] * 7 + [vmem_spec],
        out_specs=vmem_spec,
        scratch_shapes=[
            pltpu.VMEM((layers, n, CORES, n, depth // n, rank), BF16),
            pltpu.VMEM((layers, n, CORES, n, rank // n, width), BF16),
            pltpu.VMEM((n, CORES, n, depth // n, cmp), BF16),
            pltpu.VMEM((n, n, CORES) + over_weight.shape, BF16),
            pltpu.VMEM((2 * layers, n, depth // n, rank), BF16),
            pltpu.VMEM((n, depth // n, cmp), BF16),
            pltpu.VMEM((n, slot_most, n, CORES, block, emb), BF16),
            pltpu.VMEM((n_shard, slot_most, n - 1, block, emb), BF16),
            pltpu.VMEM((n_shard, slot_most, block, emb), BF16),
            pltpu.VMEM((n_shard, rows, width), BF16),
            pltpu.VMEM((n_shard, rows, width), BF16),
            pltpu.VMEM((rows, rank), F32),
            pltpu.VMEM((rows, rank), BF16),
            pltpu.VMEM((n, block, cmp), BF16),
            pltpu.VMEM((n, block, cmp), BF16),
            pltpu.VMEM(cross_bias.shape[1:], BF16),
            pltpu.VMEM(comp_bias.shape, BF16),
            pltpu.VMEM(cross_bias.shape[1:], F32),
            pltpu.VMEM((1,) + table_tower.shape, jnp.int32),
            pltpu.SMEM((1,) + table_tower.shape, jnp.int32),
            dma((1,)),
            dma((weights, n)), dma((weights, n)),
            dma((weights, n)), dma((weights, n)),
            dma((weights + 1, n)), dma((weights + 1, n)),
            dma((weights + 1, n)), dma((weights + 1, n)),
            dma((n,)), dma((n,)),
            dma((n, n)), dma((n, n)),
            dma((n, n, CORES)), dma((n, n_shard)),
            dma((n,)), dma((n,)),
            dma((2, n)), dma((2,)),
        ],
        compiler_params=pltpu.CompilerParams(
            collective_id=0, has_side_effects=True, vmem_limit_bytes=60 * 1024 * 1024
        ),
        name="towers",
    )(table_tower, table_owner, pool_view, down, up, comp, over_weight, cross_bias[0], comp_bias, over_bias)
    return result.reshape(1, block, out_width)


def solution(mesh):
    placed = (
        P("tower", None, "shard", None),
        P("tower", None, "shard", None),
        P("tower", None, None, "shard"),
        P("tower", None, None),
        P("tower", "shard", None),
        P("tower", None),
        P("tower", "shard"),
        P(),
        P(),
        P(),
    )
    towers, shards = mesh.shape["tower"], mesh.shape["shard"]
    body = turned if towers == SIDE * SIDE and towers * CORES == shards else on_device
    return jax.shard_map(
        body, mesh=mesh, in_specs=placed, out_specs=P("shard", "tower", None), check_vma=False
    )
```

```python
import jax
import jax.numpy as jnp
from jax import lax
from jax.experimental import pallas as pl
from jax.experimental.pallas import tpu as pltpu
from jax.sharding import PartitionSpec as P

MESH = pl.DeviceIdType.MESH
CORES = 2
SIDE = 2
BF16, F32 = jnp.bfloat16, jnp.float32


def slot_order(table_tower, table_owner, tower_id, per_tower, slot_most):
    table_count = table_tower.shape[0]
    index = jnp.arange(table_count, dtype=jnp.int32)
    inside = table_tower == tower_id
    earlier = index[None, :] < index[:, None]
    before = inside[None, :] & earlier
    position_in = jnp.sum(before.astype(jnp.int32), axis=1)
    same_owner = table_owner[None, :] == table_owner[:, None]
    own_slot = jnp.sum((before & same_owner).astype(jnp.int32), axis=1)
    wanted = table_owner * slot_most + own_slot
    picked = inside[None, :] & (
        position_in[None, :] == jnp.arange(per_tower, dtype=jnp.int32)[:, None]
    )
    return jnp.sum(jnp.where(picked, wanted[None, :], 0), axis=1)


def on_device(
    pooled,
    cross_down,
    cross_up,
    cross_bias,
    comp_weight,
    comp_bias,
    over_weight,
    over_bias,
    table_tower,
    table_owner,
):
    tower_id = lax.axis_index("tower")
    slot_most = pooled.shape[2]
    emb_width = pooled.shape[3]
    feature_count = cross_up.shape[3] * lax.axis_size("shard")
    per_tower = feature_count // emb_width
    received = lax.all_to_all(pooled, "shard", split_axis=1, concat_axis=2, tiled=True)
    wanted = slot_order(table_tower, table_owner, tower_id, per_tower, slot_most)
    tables = jnp.concatenate(
        [lax.dynamic_slice_in_dim(received[0], wanted[k], 1, axis=1) for k in range(per_tower)], axis=1
    )
    sample_count = tables.shape[0]
    base = tables.reshape(sample_count, feature_count)
    state = base
    for section_index in range(cross_down.shape[1]):
        current = state
        lowered = jnp.dot(
            current,
            lax.all_gather(cross_down[0, section_index], "shard", axis=0, tiled=True),
            preferred_element_type=jnp.float32,
        ).astype(jnp.bfloat16)
        raised = jnp.dot(
            lowered,
            lax.all_gather(cross_up[0, section_index], "shard", axis=1, tiled=True),
            preferred_element_type=jnp.float32,
        )
        state = (
            base.astype(jnp.float32) * (raised + cross_bias[0, section_index].astype(jnp.float32))
            + state.astype(jnp.float32)
        ).astype(jnp.bfloat16)
    squeezed = jnp.dot(
        state,
        lax.all_gather(comp_weight[0], "shard", axis=0, tiled=True),
        preferred_element_type=jnp.float32,
    )
    squeezed = (squeezed + comp_bias[0].astype(jnp.float32)).astype(jnp.bfloat16)
    tower_rows = lax.all_gather(over_weight, "shard", axis=1, tiled=True)
    summed = lax.psum_scatter(
        jnp.dot(squeezed, tower_rows, preferred_element_type=jnp.float32).astype(jnp.bfloat16),
        "tower",
        scatter_dimension=0,
        tiled=True,
    ).astype(jnp.float32)
    result = jax.nn.relu(summed + over_bias.astype(jnp.float32)).astype(jnp.bfloat16)
    return result.reshape(1, result.shape[0], result.shape[1])


def make_kernel(n, layers, tables_each, slot_most):
    weights = 2 * layers + 1

    def kernel(
        table_tower, table_owner, pooled, down, up, comp, over, cross_bias, comp_bias, over_bias, out,
        down_all, up_all, comp_all, over_all, cross_hop, comp_hop, pool_hop, received, received_last, base, state, total, lowered,
        squeezed, joined, bias, bias_low, bias_wide, order_row, wanted, order_sem,
        hop_send, hop_recv, first_send, first_recv, second_send, second_recv, core_send, core_recv,
        over_send, over_recv, pool_hop_send, pool_hop_recv, pool_send, pool_recv, mix_send, mix_recv, bias_send, bias_recv,
    ):
        t = lax.axis_index("tower")
        shard = lax.axis_index("shard")
        z, c = shard // CORES, shard % CORES
        other = 1 - c
        partner = (t, z * CORES + other)
        n_shard = n * CORES

        def remote(src, dst, send, recv, device):
            return pltpu.make_async_remote_copy(
                src_ref=src, dst_ref=dst, send_sem=send, recv_sem=recv,
                device_id=device, device_id_type=MESH,
            )

        barrier = pltpu.get_barrier_semaphore()
        for k in range(1, n):
            pl.semaphore_signal(barrier, inc=1, device_id=(lax.rem(t + k, n), shard), device_id_type=MESH)
        for k in range(1, n_shard):
            pl.semaphore_signal(barrier, inc=1, device_id=(t, lax.rem(shard + k, n_shard)), device_id_type=MESH)
        pl.semaphore_wait(barrier, n + n_shard - 2)

        pairs = []
        for layer in range(layers):
            pairs.append((down.at[layer], down_all.at[layer]))
            pairs.append((up.at[layer], up_all.at[layer]))
        pairs.append((comp, comp_all))

        def part(i, core, q):
            return over_all.at[q, :, core] if i == weights else pairs[i][1].at[:, core, q]

        def turn(k):
            return lax.rem(t + k, n)

        biases = ((cross_bias, bias), (comp_bias, bias_low))

        @pl.when(t == z)
        def _():
            for i, (source, place) in enumerate(biases):
                pltpu.make_async_copy(source, place, bias_recv.at[i]).start()
                for k in range(1, n):
                    remote(source, place, bias_send.at[i, k], bias_recv.at[i], (turn(k), shard)).start()

        def order_tables():
            count = table_tower.shape[0]
            rows_of = lax.broadcasted_iota(jnp.int32, (count, count), 0)
            cols_of = lax.broadcasted_iota(jnp.int32, (count, count), 1)

            def column(row):
                return jnp.sum(jnp.where(rows_of == cols_of, row, 0), axis=1, keepdims=True)

            owner = table_owner[...].reshape(1, count)
            inside = (table_tower[...].reshape(1, count) == z).astype(jnp.int32)
            before = jnp.where(rows_of < cols_of, column(inside), 0)
            position = jnp.sum(before, axis=0, keepdims=True)
            own_slot = jnp.sum(jnp.where(column(owner) == owner, before, 0), axis=0, keepdims=True)
            slot = owner * slot_most + own_slot
            place = jnp.where(inside == 1, position, count)
            order_row[...] = jnp.sum(
                jnp.where(column(place) == cols_of, column(slot), 0), axis=0, keepdims=True
            )
            pltpu.make_async_copy(order_row, wanted, order_sem.at[0]).start()

        def hop_of(i):
            return comp_hop if i == weights - 1 else cross_hop.at[i]

        def hop_copy(i, k):
            q = turn(k)
            return remote(
                pairs[i][0].at[q], hop_of(i).at[t], hop_send.at[i, k], hop_recv.at[i, t], (q, shard)
            )

        def hop_wait(i, k):
            tower = turn(k)
            view = hop_of(i).at[tower]
            remote(view, view, hop_send.at[i, k], hop_recv.at[i, tower], (t, shard)).wait_recv()

        def first_source(i, k):
            return pairs[i][0].at[t] if k == 0 else hop_of(i).at[turn(k)]

        def first_copy(i, k):
            return remote(
                first_source(i, k), pairs[i][1].at[z, c, t], first_send.at[i, k], first_recv.at[i, z],
                (t, turn(k) * CORES + c),
            )

        def first_local(i, k):
            return pltpu.make_async_copy(first_source(i, k), pairs[i][1].at[z, c, t], first_recv.at[i, z])

        def first_start(i, k):
            here = turn(k) == z

            @pl.when(here)
            def _():
                first_local(i, k).start()

            @pl.when(jnp.logical_not(here))
            def _():
                first_copy(i, k).start()

        def first_wait(i):
            first_local(i, 0).wait()
            for k in range(1, n):
                source = lax.rem(z + k, n)
                view = pairs[i][1].at[source, c, t]
                remote(view, view, first_send.at[i, 0], first_recv.at[i, source], (t, shard)).wait_recv()

        def over_copy(k):
            there = lax.rem(z + k, n)
            return remote(
                over, over_all.at[t, z, c], over_send.at[k], over_recv.at[z], (t, there * CORES + c)
            )

        over_local = pltpu.make_async_copy(over, over_all.at[t, z, c], over_recv.at[z])

        def over_wait():
            over_local.wait()
            for k in range(1, n):
                source = lax.rem(z + k, n)
                view = over_all.at[t, source, c]
                remote(view, view, over_send.at[k], over_recv.at[source], (t, shard)).wait_recv()

        def pool_hop_copy(h, k):
            q = turn(k)
            return remote(
                pooled.at[:, turn(1 + h), :, q], pool_hop.at[t, :, h], pool_hop_send.at[h, k], pool_hop_recv.at[h, t], (q, shard)
            )

        def pool_hop_wait(h, k):
            tower = turn(k)
            view = pool_hop.at[tower, :, h]
            remote(view, view, pool_hop_send.at[h, k], pool_hop_recv.at[h, tower], (t, shard)).wait_recv()

        def pool_source(h, k, core):
            return pooled.at[:, turn(1 + h), core, t] if k == 0 else pool_hop.at[turn(k), :, h, core]

        def pool_place(h, owner):
            return received.at[owner, :, h] if h < n - 1 else received_last.at[owner]

        def pool_copy(h, k, core):
            return remote(
                pool_source(h, k, core), pool_place(h, shard), pool_send.at[h, k, core], pool_recv.at[h, shard],
                (t, turn(k) * CORES + core),
            )

        def pool_local(h, k):
            return pltpu.make_async_copy(pool_source(h, k, c), pool_place(h, shard), pool_recv.at[h, shard])

        def pool_start(h, k):
            for core in range(CORES):
                here = jnp.logical_and(turn(k) == z, c == core)

                @pl.when(here)
                def _():
                    pool_local(h, k).start()

                @pl.when(jnp.logical_not(here))
                def _():
                    pool_copy(h, k, core).start()

        def pool_wait(h):
            pool_local(h, 0).wait()
            for k in range(1, n_shard):
                source = lax.rem(shard + k, n_shard)
                view = pool_place(h, source)
                remote(view, view, pool_send.at[h, 0, 0], pool_recv.at[h, source], (t, shard)).wait_recv()

        across, along = t % SIDE, t // SIDE
        x_next = along * SIDE + (1 - across)
        y_next = (1 - along) * SIDE + across
        diagonal = (1 - along) * SIDE + (1 - across)
        near = (t, x_next, y_next, diagonal)
        half = n // 2
        halves = (pl.ds(0, half), pl.ds(half, half))

        def second_copy(i, k):
            if k < 2:
                view = part(i, c, t)
                target = near[1 + k]
            else:
                view = part(i, c, near[k - 1]).at[halves[k - 2]]
                target = near[4 - k]
            return remote(view, view, second_send.at[i, k], second_recv.at[i, k], (target, shard))

        def second_wait(i, k):
            view = part(i, c, near[1 + k]) if k < 2 else part(i, c, diagonal).at[halves[k - 2]]
            remote(view, view, second_send.at[i, k], second_recv.at[i, k], (t, shard)).wait_recv()

        def core_copy(i, k):
            view = part(i, c, near[k])
            return remote(view, view, core_send.at[i, k], core_recv.at[i, k], partner)

        def second_start(i):
            second_copy(i, 0).start()
            second_copy(i, 1).start()
            core_copy(i, 0).start()

        def relay(i):
            for k in range(2):
                second_wait(i, k)
                second_copy(i, 2 + k).start()
                core_copy(i, 1 + k).start()

        def last(i):
            second_wait(i, 2)
            second_wait(i, 3)
            core_copy(i, 3).start()

        def complete(i):
            for k in range(n):
                view = part(i, other, near[k])
                remote(view, view, core_send.at[i, k], core_recv.at[i, k], partner).wait_recv()

        def hop_start(i):
            for k in range(1, n):
                hop_copy(i, k).start()

        def pool_hop_start(h):
            for k in range(1, n):
                pool_hop_copy(h, k).start()

        def hop_on(i):
            for k in range(1, n):
                hop_wait(i, k)
                first_start(i, k)

        def pool_on(h):
            for k in range(1, n):
                pool_hop_wait(h, k)
                pool_start(h, k)

        def spread(i):
            first_wait(i)
            second_start(i)

        rows = base.shape[1]
        width = base.shape[2]
        emb = width // tables_each
        blocks = base.shape[0]
        block = rows // n
        cmp = squeezed.shape[2]

        def gather(source, lo, hi):
            @pl.loop(0, blocks, unroll=True)
            def _(s):
                for k in range(tables_each):
                    slot = wanted[0, s * tables_each + k]
                    base[s, lo:hi, k * emb:(k + 1) * emb] = source[slot // slot_most, slot % slot_most].reshape(
                        hi - lo, emb
                    )

        def lower(layer, lo, hi):
            current = base if layer == 0 else state
            if hi - lo > rows:
                total[lo:hi, :] = jnp.zeros((hi - lo, total.shape[1]), F32)

                @pl.loop(0, blocks)
                def _(s):
                    total[lo:hi, :] += jnp.dot(
                        current[s, lo:hi, :], down_all[layer, s // CORES, s % CORES].reshape(width, -1),
                        preferred_element_type=F32,
                    )

                lowered[lo:hi, :] = total[lo:hi, :].astype(BF16)
            else:
                added = jnp.zeros((hi - lo, total.shape[1]), F32)
                for s in range(blocks):
                    added = added + jnp.dot(
                        current[s, lo:hi, :], down_all[layer, s // CORES, s % CORES].reshape(width, -1),
                        preferred_element_type=F32,
                    )
                lowered[lo:hi, :] = added.astype(BF16)

        def cross(layer, lo, hi):
            current = base if layer == 0 else state

            @pl.loop(0, blocks, unroll=True)
            def _(s):
                raised = jnp.dot(
                    lowered[lo:hi, :], up_all[layer, s // CORES, s % CORES].reshape(lowered.shape[1], width),
                    preferred_element_type=F32,
                )
                for k in range(tables_each):
                    cols = slice(k * emb, (k + 1) * emb)
                    row = bias_wide[layer:layer + 1, pl.ds(pl.multiple_of((s * tables_each + k) * emb, emb), emb)]
                    state[s, lo:hi, cols] = (
                        base[s, lo:hi, cols].astype(F32) * (raised[:, cols] + row)
                        + current[s, lo:hi, cols].astype(F32)
                    ).astype(BF16)

        def mix_copy(h):
            there = lax.rem(z + 1 + h, n)
            return remote(squeezed.at[h], joined.at[z], mix_send.at[h], mix_recv.at[z], (t, there * CORES + c))

        def squeeze(lo, hi):
            added = jnp.zeros((hi - lo, cmp), F32)
            for s in range(blocks):
                added = added + jnp.dot(
                    state[s, lo:hi, :], comp_all[s // CORES, s % CORES].reshape(width, cmp), preferred_element_type=F32
                )
            for k in range(cmp // emb):
                cols = slice(k * emb, (k + 1) * emb)
                row = bias_low[:, cols].astype(F32)
                squeezed[lo // block:hi // block, :, cols] = (
                    (added[:, cols] + row).astype(BF16).reshape((hi - lo) // block, block, emb)
                )

        def sent():
            for k in range(1, n):
                over_copy(k).wait_send()
                for h in range(n):
                    pool_hop_copy(h, k).wait_send()
                for i in range(weights):
                    hop_copy(i, k).wait_send()
            for k in range(n):
                @pl.when(turn(k) != z)
                def _():
                    for i in range(weights):
                        first_copy(i, k).wait_send()

                pool_sent(k, range(n - 1))
            for i in range(weights + 1):
                for k in range(4):
                    second_copy(i, k).wait_send()
                    if i < weights:
                        core_copy(i, k).wait_send()

            @pl.when(t == z)
            def _():
                for i, (source, place) in enumerate(biases):
                    for k in range(1, n):
                        remote(source, place, bias_send.at[i, k], bias_recv.at[i], (turn(k), shard)).wait_send()

        def pool_sent(k, chunks):
            for core in range(CORES):
                @pl.when(jnp.logical_or(turn(k) != z, c != core))
                def _():
                    for h in chunks:
                        pool_copy(h, k, core).wait_send()

        comp_id, over_id = weights - 1, weights
        early, late = (0, rows - block), (rows - block, rows)
        first_start(1, 0)
        hop_start(comp_id)
        hop_start(0)
        hop_on(comp_id)
        hop_start(3)
        first_start(0, 0)
        first_start(comp_id, 0)
        first_start(3, 0)
        hop_on(0)
        hop_start(1)
        hop_start(2)
        hop_on(1)
        pool_hop_start(0)
        hop_on(2)
        first_start(2, 0)
        hop_on(3)
        pool_start(3, 0)
        over_local.start()
        for k in range(1, n):
            over_copy(k).start()
        spread(comp_id)
        pool_hop_start(1)
        spread(0)
        pool_on(0)
        pool_start(0, 0)
        pool_start(2, 0)
        pool_hop_start(2)
        spread(1)
        pool_start(1, 0)
        spread(2)
        relay(comp_id)
        relay(0)
        pool_on(1)
        order_tables()
        pool_hop_start(3)
        spread(3)
        relay(1)
        pool_on(2)
        over_wait()
        second_start(over_id)
        relay(2)
        last(comp_id)
        relay(3)
        pool_wait(0)
        pool_on(3)
        last(1)
        pool_wait(1)
        last(0)
        pool_wait(2)
        for i, (source, place) in enumerate(biases):
            @pl.when(t == z)
            def _():
                pltpu.make_async_copy(source, place, bias_recv.at[i]).wait()

            @pl.when(t != z)
            def _():
                remote(place, place, bias_send.at[i, 0], bias_recv.at[i], (t, shard)).wait_recv()

        bias_wide[...] = bias[...].astype(F32)
        pltpu.make_async_copy(order_row, wanted, order_sem.at[0]).wait()
        gather(received, *early)
        complete(0)
        lower(0, *early)
        complete(1)
        last(2)
        cross(0, *early)
        relay(over_id)
        complete(2)
        lower(1, *early)
        last(3)
        complete(3)
        cross(1, *early)
        complete(comp_id)
        squeeze(*early)
        for h in range(n - 1):
            mix_copy(h).start()
        sent()
        pool_wait(3)
        last(over_id)
        gather(received_last, *late)
        for layer in range(layers):
            lower(layer, *late)
            cross(layer, *late)
        squeeze(*late)
        complete(over_id)
        for k in range(1, n):
            source = lax.rem(z + k, n)
            view = joined.at[source]
            remote(view, view, mix_send.at[0], mix_recv.at[source], (t, shard)).wait_recv()
        wide = over_all.shape[4]
        for s in range(n_shard):
            mixed = over_bias[s * wide:(s + 1) * wide].astype(F32).reshape(1, wide)
            for k in range(n):
                tower = lax.rem(z + k, n)
                part_in = squeezed[n - 1] if k == 0 else joined[tower]
                mixed = mixed + jnp.dot(
                    part_in, over_all[tower, s // CORES, s % CORES], preferred_element_type=F32
                )
            out[:, s * wide:(s + 1) * wide] = jnp.maximum(mixed, 0.0).astype(BF16)

        for k in range(n):
            pool_sent(k, (n - 1,))
            core_copy(weights, k).wait_send()
        for h in range(n - 1):
            mix_copy(h).wait_send()

    return kernel


def turned(
    pooled, cross_down, cross_up, cross_bias, comp_weight, comp_bias, over_weight, over_bias,
    table_tower, table_owner,
):
    n = lax.axis_size("tower")
    n_shard = lax.axis_size("shard")
    _, samples, slot_most, emb = pooled.shape
    layers, depth, rank = cross_down.shape[1:]
    width = cross_up.shape[3]
    cmp = comp_weight.shape[2]
    tables_each = width // emb
    block = samples // (n_shard * n)
    rows = n * block
    out_width = over_bias.shape[0]
    pool_view = jnp.transpose(pooled[0], (1, 0, 2)).reshape(slot_most, n, CORES, n, block, emb)
    down = cross_down[0].reshape(layers, n, depth // n, rank)
    up = cross_up[0].reshape(layers, n, rank // n, width)
    comp = comp_weight[0].reshape(n, depth // n, cmp)
    weights = 2 * layers + 1
    dma = pltpu.SemaphoreType.DMA
    any_spec = pl.BlockSpec(memory_space=pl.ANY)
    vmem_spec = pl.BlockSpec(memory_space=pltpu.VMEM)
    result = pl.pallas_call(
        make_kernel(n, layers, tables_each, slot_most),
        out_shape=jax.ShapeDtypeStruct((block, out_width), BF16),
        in_specs=[vmem_spec] * 2 + [any_spec] * 7 + [vmem_spec],
        out_specs=vmem_spec,
        scratch_shapes=[
            pltpu.VMEM((layers, n, CORES, n, depth // n, rank), BF16),
            pltpu.VMEM((layers, n, CORES, n, rank // n, width), BF16),
            pltpu.VMEM((n, CORES, n, depth // n, cmp), BF16),
            pltpu.VMEM((n, n, CORES) + over_weight.shape, BF16),
            pltpu.VMEM((2 * layers, n, depth // n, rank), BF16),
            pltpu.VMEM((n, depth // n, cmp), BF16),
            pltpu.VMEM((n, slot_most, n, CORES, block, emb), BF16),
            pltpu.VMEM((n_shard, slot_most, n - 1, block, emb), BF16),
            pltpu.VMEM((n_shard, slot_most, block, emb), BF16),
            pltpu.VMEM((n_shard, rows, width), BF16),
            pltpu.VMEM((n_shard, rows, width), BF16),
            pltpu.VMEM((rows, rank), F32),
            pltpu.VMEM((rows, rank), BF16),
            pltpu.VMEM((n, block, cmp), BF16),
            pltpu.VMEM((n, block, cmp), BF16),
            pltpu.VMEM(cross_bias.shape[1:], BF16),
            pltpu.VMEM(comp_bias.shape, BF16),
            pltpu.VMEM(cross_bias.shape[1:], F32),
            pltpu.VMEM((1,) + table_tower.shape, jnp.int32),
            pltpu.SMEM((1,) + table_tower.shape, jnp.int32),
            dma((1,)),
            dma((weights, n)), dma((weights, n)),
            dma((weights, n)), dma((weights, n)),
            dma((weights + 1, n)), dma((weights + 1, n)),
            dma((weights + 1, n)), dma((weights + 1, n)),
            dma((n,)), dma((n,)),
            dma((n, n)), dma((n, n)),
            dma((n, n, CORES)), dma((n, n_shard)),
            dma((n,)), dma((n,)),
            dma((2, n)), dma((2,)),
        ],
        compiler_params=pltpu.CompilerParams(
            collective_id=0, has_side_effects=True, vmem_limit_bytes=60 * 1024 * 1024
        ),
        name="towers",
    )(table_tower, table_owner, pool_view, down, up, comp, over_weight, cross_bias[0], comp_bias, over_bias)
    return result.reshape(1, block, out_width)


def solution(mesh):
    placed = (
        P("tower", None, "shard", None),
        P("tower", None, "shard", None),
        P("tower", None, None, "shard"),
        P("tower", None, None),
        P("tower", "shard", None),
        P("tower", None),
        P("tower", "shard"),
        P(),
        P(),
        P(),
    )
    towers, shards = mesh.shape["tower"], mesh.shape["shard"]
    body = turned if towers == SIDE * SIDE and towers * CORES == shards else on_device
    return jax.shard_map(
        body, mesh=mesh, in_specs=placed, out_specs=P("shard", "tower", None), check_vma=False
    )
```

```python
import jax
import jax.numpy as jnp
from jax import lax
from jax.experimental import pallas as pl
from jax.experimental.pallas import tpu as pltpu
from jax.sharding import PartitionSpec as P

MESH = pl.DeviceIdType.MESH
CORES = 2
SIDE = 2
BF16, F32 = jnp.bfloat16, jnp.float32


def slot_order(table_tower, table_owner, tower_id, per_tower, slot_most):
    table_count = table_tower.shape[0]
    index = jnp.arange(table_count, dtype=jnp.int32)
    inside = table_tower == tower_id
    earlier = index[None, :] < index[:, None]
    before = inside[None, :] & earlier
    position_in = jnp.sum(before.astype(jnp.int32), axis=1)
    same_owner = table_owner[None, :] == table_owner[:, None]
    own_slot = jnp.sum((before & same_owner).astype(jnp.int32), axis=1)
    wanted = table_owner * slot_most + own_slot
    picked = inside[None, :] & (
        position_in[None, :] == jnp.arange(per_tower, dtype=jnp.int32)[:, None]
    )
    return jnp.sum(jnp.where(picked, wanted[None, :], 0), axis=1)


def on_device(
    pooled,
    cross_down,
    cross_up,
    cross_bias,
    comp_weight,
    comp_bias,
    over_weight,
    over_bias,
    table_tower,
    table_owner,
):
    tower_id = lax.axis_index("tower")
    slot_most = pooled.shape[2]
    emb_width = pooled.shape[3]
    feature_count = cross_up.shape[3] * lax.axis_size("shard")
    per_tower = feature_count // emb_width
    received = lax.all_to_all(pooled, "shard", split_axis=1, concat_axis=2, tiled=True)
    wanted = slot_order(table_tower, table_owner, tower_id, per_tower, slot_most)
    tables = jnp.concatenate(
        [lax.dynamic_slice_in_dim(received[0], wanted[k], 1, axis=1) for k in range(per_tower)], axis=1
    )
    sample_count = tables.shape[0]
    base = tables.reshape(sample_count, feature_count)
    state = base
    for section_index in range(cross_down.shape[1]):
        current = state
        lowered = jnp.dot(
            current,
            lax.all_gather(cross_down[0, section_index], "shard", axis=0, tiled=True),
            preferred_element_type=jnp.float32,
        ).astype(jnp.bfloat16)
        raised = jnp.dot(
            lowered,
            lax.all_gather(cross_up[0, section_index], "shard", axis=1, tiled=True),
            preferred_element_type=jnp.float32,
        )
        state = (
            base.astype(jnp.float32) * (raised + cross_bias[0, section_index].astype(jnp.float32))
            + state.astype(jnp.float32)
        ).astype(jnp.bfloat16)
    squeezed = jnp.dot(
        state,
        lax.all_gather(comp_weight[0], "shard", axis=0, tiled=True),
        preferred_element_type=jnp.float32,
    )
    squeezed = (squeezed + comp_bias[0].astype(jnp.float32)).astype(jnp.bfloat16)
    tower_rows = lax.all_gather(over_weight, "shard", axis=1, tiled=True)
    summed = lax.psum_scatter(
        jnp.dot(squeezed, tower_rows, preferred_element_type=jnp.float32).astype(jnp.bfloat16),
        "tower",
        scatter_dimension=0,
        tiled=True,
    ).astype(jnp.float32)
    result = jax.nn.relu(summed + over_bias.astype(jnp.float32)).astype(jnp.bfloat16)
    return result.reshape(1, result.shape[0], result.shape[1])


def make_kernel(n, layers, tables_each, slot_most):
    weights = 2 * layers + 1

    def kernel(
        table_tower, table_owner, pooled, down, up, comp, over, cross_bias, comp_bias, over_bias, out,
        down_all, up_all, comp_all, over_all, cross_hop, comp_hop, pool_hop, received, received_last, base, state, total, lowered,
        squeezed, joined, bias, bias_low, bias_wide, order_row, wanted, order_sem,
        hop_send, hop_recv, first_send, first_recv, second_send, second_recv, core_send, core_recv,
        over_send, over_recv, pool_hop_send, pool_hop_recv, pool_send, pool_recv, mix_send, mix_recv, bias_send, bias_recv,
    ):
        t = lax.axis_index("tower")
        shard = lax.axis_index("shard")
        z, c = shard // CORES, shard % CORES
        other = 1 - c
        partner = (t, z * CORES + other)
        n_shard = n * CORES

        def remote(src, dst, send, recv, device):
            return pltpu.make_async_remote_copy(
                src_ref=src, dst_ref=dst, send_sem=send, recv_sem=recv,
                device_id=device, device_id_type=MESH,
            )

        barrier = pltpu.get_barrier_semaphore()
        for k in range(1, n):
            pl.semaphore_signal(barrier, inc=1, device_id=(lax.rem(t + k, n), shard), device_id_type=MESH)
        for k in range(1, n_shard):
            pl.semaphore_signal(barrier, inc=1, device_id=(t, lax.rem(shard + k, n_shard)), device_id_type=MESH)
        pl.semaphore_wait(barrier, n + n_shard - 2)

        pairs = []
        for layer in range(layers):
            pairs.append((down.at[layer], down_all.at[layer]))
            pairs.append((up.at[layer], up_all.at[layer]))
        pairs.append((comp, comp_all))

        def part(i, core, q):
            return over_all.at[q, :, core] if i == weights else pairs[i][1].at[:, core, q]

        def turn(k):
            return lax.rem(t + k, n)

        biases = ((cross_bias, bias), (comp_bias, bias_low))

        @pl.when(t == z)
        def _():
            for i, (source, place) in enumerate(biases):
                pltpu.make_async_copy(source, place, bias_recv.at[i]).start()
                for k in range(1, n):
                    remote(source, place, bias_send.at[i, k], bias_recv.at[i], (turn(k), shard)).start()

        def order_tables():
            count = table_tower.shape[0]
            rows_of = lax.broadcasted_iota(jnp.int32, (count, count), 0)
            cols_of = lax.broadcasted_iota(jnp.int32, (count, count), 1)

            def column(row):
                return jnp.sum(jnp.where(rows_of == cols_of, row, 0), axis=1, keepdims=True)

            owner = table_owner[...].reshape(1, count)
            inside = (table_tower[...].reshape(1, count) == z).astype(jnp.int32)
            before = jnp.where(rows_of < cols_of, column(inside), 0)
            position = jnp.sum(before, axis=0, keepdims=True)
            own_slot = jnp.sum(jnp.where(column(owner) == owner, before, 0), axis=0, keepdims=True)
            slot = owner * slot_most + own_slot
            place = jnp.where(inside == 1, position, count)
            order_row[...] = jnp.sum(
                jnp.where(column(place) == cols_of, column(slot), 0), axis=0, keepdims=True
            )
            pltpu.make_async_copy(order_row, wanted, order_sem.at[0]).start()

        def hop_of(i):
            return comp_hop if i == weights - 1 else cross_hop.at[i]

        def hop_copy(i, k):
            q = turn(k)
            return remote(
                pairs[i][0].at[q], hop_of(i).at[t], hop_send.at[i, k], hop_recv.at[i, t], (q, shard)
            )

        def hop_wait(i, k):
            tower = turn(k)
            view = hop_of(i).at[tower]
            remote(view, view, hop_send.at[i, k], hop_recv.at[i, tower], (t, shard)).wait_recv()

        def first_source(i, k):
            return pairs[i][0].at[t] if k == 0 else hop_of(i).at[turn(k)]

        def first_copy(i, k):
            return remote(
                first_source(i, k), pairs[i][1].at[z, c, t], first_send.at[i, k], first_recv.at[i, z],
                (t, turn(k) * CORES + c),
            )

        def first_local(i, k):
            return pltpu.make_async_copy(first_source(i, k), pairs[i][1].at[z, c, t], first_recv.at[i, z])

        def first_start(i, k):
            here = turn(k) == z

            @pl.when(here)
            def _():
                first_local(i, k).start()

            @pl.when(jnp.logical_not(here))
            def _():
                first_copy(i, k).start()

        def first_wait(i):
            first_local(i, 0).wait()
            for k in range(1, n):
                source = lax.rem(z + k, n)
                view = pairs[i][1].at[source, c, t]
                remote(view, view, first_send.at[i, 0], first_recv.at[i, source], (t, shard)).wait_recv()

        def over_copy(k):
            there = lax.rem(z + k, n)
            return remote(
                over, over_all.at[t, z, c], over_send.at[k], over_recv.at[z], (t, there * CORES + c)
            )

        over_local = pltpu.make_async_copy(over, over_all.at[t, z, c], over_recv.at[z])

        def over_wait():
            over_local.wait()
            for k in range(1, n):
                source = lax.rem(z + k, n)
                view = over_all.at[t, source, c]
                remote(view, view, over_send.at[k], over_recv.at[source], (t, shard)).wait_recv()

        def pool_hop_copy(h, k):
            q = turn(k)
            return remote(
                pooled.at[:, turn(1 + h), :, q], pool_hop.at[t, :, h], pool_hop_send.at[h, k], pool_hop_recv.at[h, t], (q, shard)
            )

        def pool_hop_wait(h, k):
            tower = turn(k)
            view = pool_hop.at[tower, :, h]
            remote(view, view, pool_hop_send.at[h, k], pool_hop_recv.at[h, tower], (t, shard)).wait_recv()

        def pool_source(h, k, core):
            return pooled.at[:, turn(1 + h), core, t] if k == 0 else pool_hop.at[turn(k), :, h, core]

        def pool_place(h, owner):
            return received.at[owner, :, h] if h < n - 1 else received_last.at[owner]

        def pool_copy(h, k, core):
            return remote(
                pool_source(h, k, core), pool_place(h, shard), pool_send.at[h, k, core], pool_recv.at[h, shard],
                (t, turn(k) * CORES + core),
            )

        def pool_local(h, k):
            return pltpu.make_async_copy(pool_source(h, k, c), pool_place(h, shard), pool_recv.at[h, shard])

        def pool_start(h, k):
            for core in range(CORES):
                here = jnp.logical_and(turn(k) == z, c == core)

                @pl.when(here)
                def _():
                    pool_local(h, k).start()

                @pl.when(jnp.logical_not(here))
                def _():
                    pool_copy(h, k, core).start()

        def pool_wait(h):
            pool_local(h, 0).wait()
            for k in range(1, n_shard):
                source = lax.rem(shard + k, n_shard)
                view = pool_place(h, source)
                remote(view, view, pool_send.at[h, 0, 0], pool_recv.at[h, source], (t, shard)).wait_recv()

        across, along = t % SIDE, t // SIDE
        x_next = along * SIDE + (1 - across)
        y_next = (1 - along) * SIDE + across
        diagonal = (1 - along) * SIDE + (1 - across)
        near = (t, x_next, y_next, diagonal)
        half = n // 2
        halves = (pl.ds(0, half), pl.ds(half, half))

        def second_copy(i, k):
            if k < 2:
                view = part(i, c, t)
                target = near[1 + k]
            else:
                view = part(i, c, near[k - 1]).at[halves[k - 2]]
                target = near[4 - k]
            return remote(view, view, second_send.at[i, k], second_recv.at[i, k], (target, shard))

        def second_wait(i, k):
            view = part(i, c, near[1 + k]) if k < 2 else part(i, c, diagonal).at[halves[k - 2]]
            remote(view, view, second_send.at[i, k], second_recv.at[i, k], (t, shard)).wait_recv()

        def core_copy(i, k):
            view = part(i, c, near[k])
            return remote(view, view, core_send.at[i, k], core_recv.at[i, k], partner)

        def second_start(i):
            second_copy(i, 0).start()
            second_copy(i, 1).start()
            core_copy(i, 0).start()

        def relay(i):
            for k in range(2):
                second_wait(i, k)
                second_copy(i, 2 + k).start()
                core_copy(i, 1 + k).start()

        def last(i):
            second_wait(i, 2)
            second_wait(i, 3)
            core_copy(i, 3).start()

        def complete(i):
            for k in range(n):
                view = part(i, other, near[k])
                remote(view, view, core_send.at[i, k], core_recv.at[i, k], partner).wait_recv()

        def hop_start(i):
            for k in range(1, n):
                hop_copy(i, k).start()

        def pool_hop_start(h):
            for k in range(1, n):
                pool_hop_copy(h, k).start()

        def hop_on(i):
            for k in range(1, n):
                hop_wait(i, k)
                first_start(i, k)

        def pool_on(h):
            for k in range(1, n):
                pool_hop_wait(h, k)
                pool_start(h, k)

        def spread(i):
            first_wait(i)
            second_start(i)

        rows = base.shape[1]
        width = base.shape[2]
        emb = width // tables_each
        blocks = base.shape[0]
        block = rows // n
        cmp = squeezed.shape[2]

        def gather(source, lo, hi):
            @pl.loop(0, blocks, unroll=True)
            def _(s):
                for k in range(tables_each):
                    slot = wanted[0, s * tables_each + k]
                    base[s, lo:hi, k * emb:(k + 1) * emb] = source[slot // slot_most, slot % slot_most].reshape(
                        hi - lo, emb
                    )

        def lower(layer, lo, hi):
            current = base if layer == 0 else state
            if hi - lo > rows:
                total[lo:hi, :] = jnp.zeros((hi - lo, total.shape[1]), F32)

                @pl.loop(0, blocks)
                def _(s):
                    total[lo:hi, :] += jnp.dot(
                        current[s, lo:hi, :], down_all[layer, s // CORES, s % CORES].reshape(width, -1),
                        preferred_element_type=F32,
                    )

                lowered[lo:hi, :] = total[lo:hi, :].astype(BF16)
            else:
                added = jnp.zeros((hi - lo, total.shape[1]), F32)
                for s in range(blocks):
                    added = added + jnp.dot(
                        current[s, lo:hi, :], down_all[layer, s // CORES, s % CORES].reshape(width, -1),
                        preferred_element_type=F32,
                    )
                lowered[lo:hi, :] = added.astype(BF16)

        def cross(layer, lo, hi):
            current = base if layer == 0 else state

            added = jnp.zeros((hi - lo, cmp), F32)
            for s in range(blocks):
                raised = jnp.dot(
                    lowered[lo:hi, :], up_all[layer, s // CORES, s % CORES].reshape(lowered.shape[1], width),
                    preferred_element_type=F32,
                )
                for k in range(tables_each):
                    cols = slice(k * emb, (k + 1) * emb)
                    row = bias_wide[layer:layer + 1, pl.ds(pl.multiple_of((s * tables_each + k) * emb, emb), emb)]
                    state[s, lo:hi, cols] = (
                        base[s, lo:hi, cols].astype(F32) * (raised[:, cols] + row)
                        + current[s, lo:hi, cols].astype(F32)
                    ).astype(BF16)
                if layer == layers - 1:
                    added = added + jnp.dot(
                        state[s, lo:hi, :], comp_all[s // CORES, s % CORES].reshape(width, cmp),
                        preferred_element_type=F32,
                    )
            return added

        def mix_copy(h):
            there = lax.rem(z + 1 + h, n)
            return remote(squeezed.at[h], joined.at[z], mix_send.at[h], mix_recv.at[z], (t, there * CORES + c))

        def squeeze(lo, hi, added):
            for k in range(cmp // emb):
                cols = slice(k * emb, (k + 1) * emb)
                row = bias_low[:, cols].astype(F32)
                squeezed[lo // block:hi // block, :, cols] = (
                    (added[:, cols] + row).astype(BF16).reshape((hi - lo) // block, block, emb)
                )

        def sent():
            for k in range(1, n):
                over_copy(k).wait_send()
                for h in range(n):
                    pool_hop_copy(h, k).wait_send()
                for i in range(weights):
                    hop_copy(i, k).wait_send()
            for k in range(n):
                @pl.when(turn(k) != z)
                def _():
                    for i in range(weights):
                        first_copy(i, k).wait_send()

                pool_sent(k, range(n - 1))
            for i in range(weights + 1):
                for k in range(4):
                    second_copy(i, k).wait_send()
                    if i < weights:
                        core_copy(i, k).wait_send()

            @pl.when(t == z)
            def _():
                for i, (source, place) in enumerate(biases):
                    for k in range(1, n):
                        remote(source, place, bias_send.at[i, k], bias_recv.at[i], (turn(k), shard)).wait_send()

        def pool_sent(k, chunks):
            for core in range(CORES):
                @pl.when(jnp.logical_or(turn(k) != z, c != core))
                def _():
                    for h in chunks:
                        pool_copy(h, k, core).wait_send()

        comp_id, over_id = weights - 1, weights
        early, late = (0, rows - block), (rows - block, rows)
        first_start(1, 0)
        hop_start(comp_id)
        hop_start(0)
        hop_on(comp_id)
        hop_start(3)
        first_start(0, 0)
        first_start(comp_id, 0)
        first_start(3, 0)
        hop_on(0)
        hop_start(1)
        hop_start(2)
        hop_on(1)
        pool_hop_start(0)
        hop_on(2)
        first_start(2, 0)
        hop_on(3)
        pool_start(3, 0)
        over_local.start()
        for k in range(1, n):
            over_copy(k).start()
        spread(comp_id)
        pool_hop_start(1)
        spread(0)
        pool_on(0)
        pool_start(0, 0)
        pool_start(2, 0)
        pool_hop_start(2)
        spread(1)
        pool_start(1, 0)
        spread(2)
        relay(comp_id)
        relay(0)
        pool_on(1)
        order_tables()
        pool_hop_start(3)
        spread(3)
        relay(1)
        pool_on(2)
        over_wait()
        second_start(over_id)
        relay(2)
        last(comp_id)
        relay(3)
        pool_wait(0)
        pool_on(3)
        last(1)
        pool_wait(1)
        last(0)
        pool_wait(2)
        for i, (source, place) in enumerate(biases):
            @pl.when(t == z)
            def _():
                pltpu.make_async_copy(source, place, bias_recv.at[i]).wait()

            @pl.when(t != z)
            def _():
                remote(place, place, bias_send.at[i, 0], bias_recv.at[i], (t, shard)).wait_recv()

        bias_wide[...] = bias[...].astype(F32)
        pltpu.make_async_copy(order_row, wanted, order_sem.at[0]).wait()
        gather(received, *early)
        complete(0)
        lower(0, *early)
        complete(1)
        last(2)
        cross(0, *early)
        relay(over_id)
        complete(2)
        lower(1, *early)
        last(3)
        complete(3)
        complete(comp_id)
        squeeze(*early, cross(1, *early))
        for h in range(n - 1):
            mix_copy(h).start()
        sent()
        pool_wait(3)
        last(over_id)
        gather(received_last, *late)
        for layer in range(layers):
            lower(layer, *late)
            added = cross(layer, *late)
        squeeze(*late, added)
        complete(over_id)
        for k in range(1, n):
            source = lax.rem(z + k, n)
            view = joined.at[source]
            remote(view, view, mix_send.at[0], mix_recv.at[source], (t, shard)).wait_recv()
        wide = over_all.shape[4]
        for s in range(n_shard):
            mixed = over_bias[s * wide:(s + 1) * wide].astype(F32).reshape(1, wide)
            for k in range(n):
                tower = lax.rem(z + k, n)
                part_in = squeezed[n - 1] if k == 0 else joined[tower]
                mixed = mixed + jnp.dot(
                    part_in, over_all[tower, s // CORES, s % CORES], preferred_element_type=F32
                )
            out[:, s * wide:(s + 1) * wide] = jnp.maximum(mixed, 0.0).astype(BF16)

        for k in range(n):
            pool_sent(k, (n - 1,))
            core_copy(weights, k).wait_send()
        for h in range(n - 1):
            mix_copy(h).wait_send()

    return kernel


def turned(
    pooled, cross_down, cross_up, cross_bias, comp_weight, comp_bias, over_weight, over_bias,
    table_tower, table_owner,
):
    n = lax.axis_size("tower")
    n_shard = lax.axis_size("shard")
    _, samples, slot_most, emb = pooled.shape
    layers, depth, rank = cross_down.shape[1:]
    width = cross_up.shape[3]
    cmp = comp_weight.shape[2]
    tables_each = width // emb
    block = samples // (n_shard * n)
    rows = n * block
    out_width = over_bias.shape[0]
    pool_view = jnp.transpose(pooled[0], (1, 0, 2)).reshape(slot_most, n, CORES, n, block, emb)
    down = cross_down[0].reshape(layers, n, depth // n, rank)
    up = cross_up[0].reshape(layers, n, rank // n, width)
    comp = comp_weight[0].reshape(n, depth // n, cmp)
    weights = 2 * layers + 1
    dma = pltpu.SemaphoreType.DMA
    any_spec = pl.BlockSpec(memory_space=pl.ANY)
    vmem_spec = pl.BlockSpec(memory_space=pltpu.VMEM)
    result = pl.pallas_call(
        make_kernel(n, layers, tables_each, slot_most),
        out_shape=jax.ShapeDtypeStruct((block, out_width), BF16),
        in_specs=[vmem_spec] * 2 + [any_spec] * 7 + [vmem_spec],
        out_specs=vmem_spec,
        scratch_shapes=[
            pltpu.VMEM((layers, n, CORES, n, depth // n, rank), BF16),
            pltpu.VMEM((layers, n, CORES, n, rank // n, width), BF16),
            pltpu.VMEM((n, CORES, n, depth // n, cmp), BF16),
            pltpu.VMEM((n, n, CORES) + over_weight.shape, BF16),
            pltpu.VMEM((2 * layers, n, depth // n, rank), BF16),
            pltpu.VMEM((n, depth // n, cmp), BF16),
            pltpu.VMEM((n, slot_most, n, CORES, block, emb), BF16),
            pltpu.VMEM((n_shard, slot_most, n - 1, block, emb), BF16),
            pltpu.VMEM((n_shard, slot_most, block, emb), BF16),
            pltpu.VMEM((n_shard, rows, width), BF16),
            pltpu.VMEM((n_shard, rows, width), BF16),
            pltpu.VMEM((rows, rank), F32),
            pltpu.VMEM((rows, rank), BF16),
            pltpu.VMEM((n, block, cmp), BF16),
            pltpu.VMEM((n, block, cmp), BF16),
            pltpu.VMEM(cross_bias.shape[1:], BF16),
            pltpu.VMEM(comp_bias.shape, BF16),
            pltpu.VMEM(cross_bias.shape[1:], F32),
            pltpu.VMEM((1,) + table_tower.shape, jnp.int32),
            pltpu.SMEM((1,) + table_tower.shape, jnp.int32),
            dma((1,)),
            dma((weights, n)), dma((weights, n)),
            dma((weights, n)), dma((weights, n)),
            dma((weights + 1, n)), dma((weights + 1, n)),
            dma((weights + 1, n)), dma((weights + 1, n)),
            dma((n,)), dma((n,)),
            dma((n, n)), dma((n, n)),
            dma((n, n, CORES)), dma((n, n_shard)),
            dma((n,)), dma((n,)),
            dma((2, n)), dma((2,)),
        ],
        compiler_params=pltpu.CompilerParams(
            collective_id=0, has_side_effects=True, vmem_limit_bytes=60 * 1024 * 1024
        ),
        name="towers",
    )(table_tower, table_owner, pool_view, down, up, comp, over_weight, cross_bias[0], comp_bias, over_bias)
    return result.reshape(1, block, out_width)


def solution(mesh):
    placed = (
        P("tower", None, "shard", None),
        P("tower", None, "shard", None),
        P("tower", None, None, "shard"),
        P("tower", None, None),
        P("tower", "shard", None),
        P("tower", None),
        P("tower", "shard"),
        P(),
        P(),
        P(),
    )
    towers, shards = mesh.shape["tower"], mesh.shape["shard"]
    body = turned if towers == SIDE * SIDE and towers * CORES == shards else on_device
    return jax.shard_map(
        body, mesh=mesh, in_specs=placed, out_specs=P("shard", "tower", None), check_vma=False
    )
```

```python
import jax
import jax.numpy as jnp
from jax import lax
from jax.experimental import pallas as pl
from jax.experimental.pallas import tpu as pltpu
from jax.sharding import PartitionSpec as P

MESH = pl.DeviceIdType.MESH
CORES = 2
SIDE = 2
BF16, F32 = jnp.bfloat16, jnp.float32


def slot_order(table_tower, table_owner, tower_id, per_tower, slot_most):
    table_count = table_tower.shape[0]
    index = jnp.arange(table_count, dtype=jnp.int32)
    inside = table_tower == tower_id
    earlier = index[None, :] < index[:, None]
    before = inside[None, :] & earlier
    position_in = jnp.sum(before.astype(jnp.int32), axis=1)
    same_owner = table_owner[None, :] == table_owner[:, None]
    own_slot = jnp.sum((before & same_owner).astype(jnp.int32), axis=1)
    wanted = table_owner * slot_most + own_slot
    picked = inside[None, :] & (
        position_in[None, :] == jnp.arange(per_tower, dtype=jnp.int32)[:, None]
    )
    return jnp.sum(jnp.where(picked, wanted[None, :], 0), axis=1)


def on_device(
    pooled,
    cross_down,
    cross_up,
    cross_bias,
    comp_weight,
    comp_bias,
    over_weight,
    over_bias,
    table_tower,
    table_owner,
):
    tower_id = lax.axis_index("tower")
    slot_most = pooled.shape[2]
    emb_width = pooled.shape[3]
    feature_count = cross_up.shape[3] * lax.axis_size("shard")
    per_tower = feature_count // emb_width
    received = lax.all_to_all(pooled, "shard", split_axis=1, concat_axis=2, tiled=True)
    wanted = slot_order(table_tower, table_owner, tower_id, per_tower, slot_most)
    tables = jnp.concatenate(
        [lax.dynamic_slice_in_dim(received[0], wanted[k], 1, axis=1) for k in range(per_tower)], axis=1
    )
    sample_count = tables.shape[0]
    base = tables.reshape(sample_count, feature_count)
    state = base
    for section_index in range(cross_down.shape[1]):
        current = state
        lowered = jnp.dot(
            current,
            lax.all_gather(cross_down[0, section_index], "shard", axis=0, tiled=True),
            preferred_element_type=jnp.float32,
        ).astype(jnp.bfloat16)
        raised = jnp.dot(
            lowered,
            lax.all_gather(cross_up[0, section_index], "shard", axis=1, tiled=True),
            preferred_element_type=jnp.float32,
        )
        state = (
            base.astype(jnp.float32) * (raised + cross_bias[0, section_index].astype(jnp.float32))
            + state.astype(jnp.float32)
        ).astype(jnp.bfloat16)
    squeezed = jnp.dot(
        state,
        lax.all_gather(comp_weight[0], "shard", axis=0, tiled=True),
        preferred_element_type=jnp.float32,
    )
    squeezed = (squeezed + comp_bias[0].astype(jnp.float32)).astype(jnp.bfloat16)
    tower_rows = lax.all_gather(over_weight, "shard", axis=1, tiled=True)
    summed = lax.psum_scatter(
        jnp.dot(squeezed, tower_rows, preferred_element_type=jnp.float32).astype(jnp.bfloat16),
        "tower",
        scatter_dimension=0,
        tiled=True,
    ).astype(jnp.float32)
    result = jax.nn.relu(summed + over_bias.astype(jnp.float32)).astype(jnp.bfloat16)
    return result.reshape(1, result.shape[0], result.shape[1])


def make_kernel(n, layers, tables_each, slot_most):
    weights = 2 * layers + 1

    def kernel(
        table_tower, table_owner, pooled, down, up, comp, over, cross_bias, comp_bias, over_bias, out,
        down_all, up_all, comp_all, over_all, cross_hop, comp_hop, pool_hop, received, received_last, base, state, total, lowered,
        squeezed, joined, bias, bias_low, bias_wide, order_row, wanted, order_sem,
        hop_send, hop_recv, first_send, first_recv, second_send, second_recv, core_send, core_recv,
        over_send, over_recv, pool_hop_send, pool_hop_recv, pool_send, pool_recv, mix_send, mix_recv, bias_send, bias_recv,
    ):
        t = lax.axis_index("tower")
        shard = lax.axis_index("shard")
        z, c = shard // CORES, shard % CORES
        other = 1 - c
        partner = (t, z * CORES + other)
        n_shard = n * CORES

        def remote(src, dst, send, recv, device):
            return pltpu.make_async_remote_copy(
                src_ref=src, dst_ref=dst, send_sem=send, recv_sem=recv,
                device_id=device, device_id_type=MESH,
            )

        barrier = pltpu.get_barrier_semaphore()
        for k in range(1, n):
            pl.semaphore_signal(barrier, inc=1, device_id=(lax.rem(t + k, n), shard), device_id_type=MESH)
        for k in range(1, n_shard):
            pl.semaphore_signal(barrier, inc=1, device_id=(t, lax.rem(shard + k, n_shard)), device_id_type=MESH)
        pl.semaphore_wait(barrier, n + n_shard - 2)

        pairs = []
        for layer in range(layers):
            pairs.append((down.at[layer], down_all.at[layer]))
            pairs.append((up.at[layer], up_all.at[layer]))
        pairs.append((comp, comp_all))

        def part(i, core, q):
            return over_all.at[q, :, core] if i == weights else pairs[i][1].at[:, core, q]

        def turn(k):
            return lax.rem(t + k, n)

        biases = ((cross_bias, bias), (comp_bias, bias_low))

        @pl.when(t == z)
        def _():
            for i, (source, place) in enumerate(biases):
                pltpu.make_async_copy(source, place, bias_recv.at[i]).start()
                for k in range(1, n):
                    remote(source, place, bias_send.at[i, k], bias_recv.at[i], (turn(k), shard)).start()

        def order_tables():
            count = table_tower.shape[0]
            rows_of = lax.broadcasted_iota(jnp.int32, (count, count), 0)
            cols_of = lax.broadcasted_iota(jnp.int32, (count, count), 1)

            def column(row):
                return jnp.sum(jnp.where(rows_of == cols_of, row, 0), axis=1, keepdims=True)

            owner = table_owner[...].reshape(1, count)
            inside = (table_tower[...].reshape(1, count) == z).astype(jnp.int32)
            before = jnp.where(rows_of < cols_of, column(inside), 0)
            position = jnp.sum(before, axis=0, keepdims=True)
            own_slot = jnp.sum(jnp.where(column(owner) == owner, before, 0), axis=0, keepdims=True)
            slot = owner * slot_most + own_slot
            place = jnp.where(inside == 1, position, count)
            order_row[...] = jnp.sum(
                jnp.where(column(place) == cols_of, column(slot), 0), axis=0, keepdims=True
            )
            pltpu.make_async_copy(order_row, wanted, order_sem.at[0]).start()

        def hop_of(i):
            return comp_hop if i == weights - 1 else cross_hop.at[i]

        def hop_copy(i, k):
            q = turn(k)
            return remote(
                pairs[i][0].at[q], hop_of(i).at[t], hop_send.at[i, k], hop_recv.at[i, t], (q, shard)
            )

        def hop_wait(i, k):
            tower = turn(k)
            view = hop_of(i).at[tower]
            remote(view, view, hop_send.at[i, k], hop_recv.at[i, tower], (t, shard)).wait_recv()

        def first_source(i, k):
            return pairs[i][0].at[t] if k == 0 else hop_of(i).at[turn(k)]

        def first_copy(i, k):
            return remote(
                first_source(i, k), pairs[i][1].at[z, c, t], first_send.at[i, k], first_recv.at[i, z],
                (t, turn(k) * CORES + c),
            )

        def first_local(i, k):
            return pltpu.make_async_copy(first_source(i, k), pairs[i][1].at[z, c, t], first_recv.at[i, z])

        def first_start(i, k):
            here = turn(k) == z

            @pl.when(here)
            def _():
                first_local(i, k).start()

            @pl.when(jnp.logical_not(here))
            def _():
                first_copy(i, k).start()

        def first_wait(i):
            first_local(i, 0).wait()
            for k in range(1, n):
                source = lax.rem(z + k, n)
                view = pairs[i][1].at[source, c, t]
                remote(view, view, first_send.at[i, 0], first_recv.at[i, source], (t, shard)).wait_recv()

        def over_copy(k):
            there = lax.rem(z + k, n)
            return remote(
                over, over_all.at[t, z, c], over_send.at[k], over_recv.at[z], (t, there * CORES + c)
            )

        over_local = pltpu.make_async_copy(over, over_all.at[t, z, c], over_recv.at[z])

        def over_wait():
            over_local.wait()
            for k in range(1, n):
                source = lax.rem(z + k, n)
                view = over_all.at[t, source, c]
                remote(view, view, over_send.at[k], over_recv.at[source], (t, shard)).wait_recv()

        def pool_hop_copy(h, k):
            q = turn(k)
            return remote(
                pooled.at[:, turn(1 + h), :, q], pool_hop.at[t, :, h], pool_hop_send.at[h, k], pool_hop_recv.at[h, t], (q, shard)
            )

        def pool_hop_wait(h, k):
            tower = turn(k)
            view = pool_hop.at[tower, :, h]
            remote(view, view, pool_hop_send.at[h, k], pool_hop_recv.at[h, tower], (t, shard)).wait_recv()

        def pool_source(h, k, core):
            return pooled.at[:, turn(1 + h), core, t] if k == 0 else pool_hop.at[turn(k), :, h, core]

        def pool_place(h, owner):
            return received.at[owner, :, h] if h < n - 1 else received_last.at[owner]

        def pool_copy(h, k, core):
            return remote(
                pool_source(h, k, core), pool_place(h, shard), pool_send.at[h, k, core], pool_recv.at[h, shard],
                (t, turn(k) * CORES + core),
            )

        def pool_local(h, k):
            return pltpu.make_async_copy(pool_source(h, k, c), pool_place(h, shard), pool_recv.at[h, shard])

        def pool_start(h, k):
            for core in range(CORES):
                here = jnp.logical_and(turn(k) == z, c == core)

                @pl.when(here)
                def _():
                    pool_local(h, k).start()

                @pl.when(jnp.logical_not(here))
                def _():
                    pool_copy(h, k, core).start()

        def pool_wait(h):
            pool_local(h, 0).wait()
            for k in range(1, n_shard):
                source = lax.rem(shard + k, n_shard)
                view = pool_place(h, source)
                remote(view, view, pool_send.at[h, 0, 0], pool_recv.at[h, source], (t, shard)).wait_recv()

        across, along = t % SIDE, t // SIDE
        x_next = along * SIDE + (1 - across)
        y_next = (1 - along) * SIDE + across
        diagonal = (1 - along) * SIDE + (1 - across)
        near = (t, x_next, y_next, diagonal)
        half = n // 2
        halves = (pl.ds(0, half), pl.ds(half, half))

        def second_copy(i, k):
            if k < 2:
                view = part(i, c, t)
                target = near[1 + k]
            else:
                view = part(i, c, near[k - 1]).at[halves[k - 2]]
                target = near[4 - k]
            return remote(view, view, second_send.at[i, k], second_recv.at[i, k], (target, shard))

        def second_wait(i, k):
            view = part(i, c, near[1 + k]) if k < 2 else part(i, c, diagonal).at[halves[k - 2]]
            remote(view, view, second_send.at[i, k], second_recv.at[i, k], (t, shard)).wait_recv()

        def core_copy(i, k):
            view = part(i, c, near[k])
            return remote(view, view, core_send.at[i, k], core_recv.at[i, k], partner)

        def second_start(i):
            second_copy(i, 0).start()
            second_copy(i, 1).start()
            core_copy(i, 0).start()

        def relay(i):
            for k in range(2):
                second_wait(i, k)
                second_copy(i, 2 + k).start()
                core_copy(i, 1 + k).start()

        def last(i):
            second_wait(i, 2)
            second_wait(i, 3)
            core_copy(i, 3).start()

        def complete(i):
            for k in range(n):
                view = part(i, other, near[k])
                remote(view, view, core_send.at[i, k], core_recv.at[i, k], partner).wait_recv()

        def hop_start(i):
            for k in range(1, n):
                hop_copy(i, k).start()

        def pool_hop_start(h):
            for k in range(1, n):
                pool_hop_copy(h, k).start()

        def hop_on(i):
            for k in range(1, n):
                hop_wait(i, k)
                first_start(i, k)

        def pool_on(h):
            for k in range(1, n):
                pool_hop_wait(h, k)
                pool_start(h, k)

        def spread(i):
            first_wait(i)
            second_start(i)

        rows = base.shape[1]
        width = base.shape[2]
        emb = width // tables_each
        blocks = base.shape[0]
        block = rows // n
        cmp = squeezed.shape[2]

        def gather(source, lo, hi):
            @pl.loop(0, blocks, unroll=True)
            def _(s):
                for k in range(tables_each):
                    slot = wanted[0, s * tables_each + k]
                    base[s, lo:hi, k * emb:(k + 1) * emb] = source[slot // slot_most, slot % slot_most].reshape(
                        hi - lo, emb
                    )

        def lower(layer, lo, hi):
            current = base if layer == 0 else state
            if hi - lo > rows:
                total[lo:hi, :] = jnp.zeros((hi - lo, total.shape[1]), F32)

                @pl.loop(0, blocks)
                def _(s):
                    total[lo:hi, :] += jnp.dot(
                        current[s, lo:hi, :], down_all[layer, s // CORES, s % CORES].reshape(width, -1),
                        preferred_element_type=F32,
                    )

                lowered[lo:hi, :] = total[lo:hi, :].astype(BF16)
            else:
                added = jnp.zeros((hi - lo, total.shape[1]), F32)
                for s in range(blocks):
                    added = added + jnp.dot(
                        current[s, lo:hi, :], down_all[layer, s // CORES, s % CORES].reshape(width, -1),
                        preferred_element_type=F32,
                    )
                lowered[lo:hi, :] = added.astype(BF16)

        def cross(layer, lo, hi):
            current = base if layer == 0 else state

            added = jnp.zeros((hi - lo, cmp), F32)
            for s in range(blocks):
                raised = jnp.dot(
                    lowered[lo:hi, :], up_all[layer, s // CORES, s % CORES].reshape(lowered.shape[1], width),
                    preferred_element_type=F32,
                )
                for k in range(tables_each):
                    cols = slice(k * emb, (k + 1) * emb)
                    row = bias_wide[layer:layer + 1, pl.ds(pl.multiple_of((s * tables_each + k) * emb, emb), emb)]
                    state[s, lo:hi, cols] = (
                        base[s, lo:hi, cols].astype(F32) * (raised[:, cols] + row)
                        + current[s, lo:hi, cols].astype(F32)
                    ).astype(BF16)
                if layer == layers - 1:
                    added = added + jnp.dot(
                        state[s, lo:hi, :], comp_all[s // CORES, s % CORES].reshape(width, cmp),
                        preferred_element_type=F32,
                    )
            return added

        def mix_copy(h):
            there = lax.rem(z + 1 + h, n)
            return remote(squeezed.at[h], joined.at[z], mix_send.at[h], mix_recv.at[z], (t, there * CORES + c))

        def squeeze(lo, hi, added):
            for k in range(cmp // emb):
                cols = slice(k * emb, (k + 1) * emb)
                row = bias_low[:, cols].astype(F32)
                squeezed[lo // block:hi // block, :, cols] = (
                    (added[:, cols] + row).astype(BF16).reshape((hi - lo) // block, block, emb)
                )

        def sent():
            for k in range(1, n):
                over_copy(k).wait_send()
                for h in range(n):
                    pool_hop_copy(h, k).wait_send()
                for i in range(weights):
                    hop_copy(i, k).wait_send()
            for k in range(n):
                @pl.when(turn(k) != z)
                def _():
                    for i in range(weights):
                        first_copy(i, k).wait_send()

                pool_sent(k, range(n - 1))
            for i in range(weights + 1):
                for k in range(4):
                    second_copy(i, k).wait_send()
                    if i < weights:
                        core_copy(i, k).wait_send()

            @pl.when(t == z)
            def _():
                for i, (source, place) in enumerate(biases):
                    for k in range(1, n):
                        remote(source, place, bias_send.at[i, k], bias_recv.at[i], (turn(k), shard)).wait_send()

        def pool_sent(k, chunks):
            for core in range(CORES):
                @pl.when(jnp.logical_or(turn(k) != z, c != core))
                def _():
                    for h in chunks:
                        pool_copy(h, k, core).wait_send()

        comp_id, over_id = weights - 1, weights
        early, late = (0, rows - block), (rows - block, rows)
        first_start(1, 0)
        hop_start(comp_id)
        hop_start(0)
        hop_on(comp_id)
        hop_start(3)
        first_start(0, 0)
        first_start(comp_id, 0)
        first_start(3, 0)
        hop_on(0)
        hop_start(1)
        hop_start(2)
        hop_on(1)
        pool_hop_start(0)
        hop_on(2)
        first_start(2, 0)
        hop_on(3)
        pool_start(3, 0)
        over_local.start()
        for k in range(1, n):
            over_copy(k).start()
        spread(comp_id)
        pool_hop_start(1)
        spread(0)
        pool_on(0)
        pool_start(0, 0)
        pool_start(2, 0)
        pool_hop_start(2)
        spread(1)
        pool_start(1, 0)
        spread(2)
        relay(comp_id)
        relay(0)
        pool_on(1)
        order_tables()
        pool_hop_start(3)
        spread(3)
        relay(1)
        pool_on(2)
        over_wait()
        second_start(over_id)
        relay(2)
        last(comp_id)
        relay(3)
        pool_wait(0)
        pool_on(3)
        last(1)
        pool_wait(1)
        last(0)
        pool_wait(2)
        for i, (source, place) in enumerate(biases):
            @pl.when(t == z)
            def _():
                pltpu.make_async_copy(source, place, bias_recv.at[i]).wait()

            @pl.when(t != z)
            def _():
                remote(place, place, bias_send.at[i, 0], bias_recv.at[i], (t, shard)).wait_recv()

        bias_wide[...] = bias[...].astype(F32)
        pltpu.make_async_copy(order_row, wanted, order_sem.at[0]).wait()
        gather(received, *early)
        complete(0)
        lower(0, *early)
        complete(1)
        last(2)
        cross(0, *early)
        relay(over_id)
        complete(2)
        lower(1, *early)
        last(3)
        complete(3)
        complete(comp_id)
        squeeze(*early, cross(1, *early))
        for h in range(n - 1):
            mix_copy(h).start()
        sent()
        pool_wait(3)
        last(over_id)
        gather(received_last, *late)
        for layer in range(layers):
            lower(layer, *late)
            added = cross(layer, *late)
        squeeze(*late, added)
        complete(over_id)
        wide = over_all.shape[4]
        begun = [
            over_bias[s * wide:(s + 1) * wide].astype(F32).reshape(1, wide)
            + jnp.dot(squeezed[n - 1], over_all[z, s // CORES, s % CORES], preferred_element_type=F32)
            for s in range(n_shard)
        ]
        for k in range(1, n):
            source = lax.rem(z + k, n)
            view = joined.at[source]
            remote(view, view, mix_send.at[0], mix_recv.at[source], (t, shard)).wait_recv()
        for s in range(n_shard):
            mixed = begun[s]
            for k in range(1, n):
                tower = lax.rem(z + k, n)
                mixed = mixed + jnp.dot(
                    joined[tower], over_all[tower, s // CORES, s % CORES], preferred_element_type=F32
                )
            out[:, s * wide:(s + 1) * wide] = jnp.maximum(mixed, 0.0).astype(BF16)

        for k in range(n):
            pool_sent(k, (n - 1,))
            core_copy(weights, k).wait_send()
        for h in range(n - 1):
            mix_copy(h).wait_send()

    return kernel


def turned(
    pooled, cross_down, cross_up, cross_bias, comp_weight, comp_bias, over_weight, over_bias,
    table_tower, table_owner,
):
    n = lax.axis_size("tower")
    n_shard = lax.axis_size("shard")
    _, samples, slot_most, emb = pooled.shape
    layers, depth, rank = cross_down.shape[1:]
    width = cross_up.shape[3]
    cmp = comp_weight.shape[2]
    tables_each = width // emb
    block = samples // (n_shard * n)
    rows = n * block
    out_width = over_bias.shape[0]
    pool_view = jnp.transpose(pooled[0], (1, 0, 2)).reshape(slot_most, n, CORES, n, block, emb)
    down = cross_down[0].reshape(layers, n, depth // n, rank)
    up = cross_up[0].reshape(layers, n, rank // n, width)
    comp = comp_weight[0].reshape(n, depth // n, cmp)
    weights = 2 * layers + 1
    dma = pltpu.SemaphoreType.DMA
    any_spec = pl.BlockSpec(memory_space=pl.ANY)
    vmem_spec = pl.BlockSpec(memory_space=pltpu.VMEM)
    result = pl.pallas_call(
        make_kernel(n, layers, tables_each, slot_most),
        out_shape=jax.ShapeDtypeStruct((block, out_width), BF16),
        in_specs=[vmem_spec] * 2 + [any_spec] * 7 + [vmem_spec],
        out_specs=vmem_spec,
        scratch_shapes=[
            pltpu.VMEM((layers, n, CORES, n, depth // n, rank), BF16),
            pltpu.VMEM((layers, n, CORES, n, rank // n, width), BF16),
            pltpu.VMEM((n, CORES, n, depth // n, cmp), BF16),
            pltpu.VMEM((n, n, CORES) + over_weight.shape, BF16),
            pltpu.VMEM((2 * layers, n, depth // n, rank), BF16),
            pltpu.VMEM((n, depth // n, cmp), BF16),
            pltpu.VMEM((n, slot_most, n, CORES, block, emb), BF16),
            pltpu.VMEM((n_shard, slot_most, n - 1, block, emb), BF16),
            pltpu.VMEM((n_shard, slot_most, block, emb), BF16),
            pltpu.VMEM((n_shard, rows, width), BF16),
            pltpu.VMEM((n_shard, rows, width), BF16),
            pltpu.VMEM((rows, rank), F32),
            pltpu.VMEM((rows, rank), BF16),
            pltpu.VMEM((n, block, cmp), BF16),
            pltpu.VMEM((n, block, cmp), BF16),
            pltpu.VMEM(cross_bias.shape[1:], BF16),
            pltpu.VMEM(comp_bias.shape, BF16),
            pltpu.VMEM(cross_bias.shape[1:], F32),
            pltpu.VMEM((1,) + table_tower.shape, jnp.int32),
            pltpu.SMEM((1,) + table_tower.shape, jnp.int32),
            dma((1,)),
            dma((weights, n)), dma((weights, n)),
            dma((weights, n)), dma((weights, n)),
            dma((weights + 1, n)), dma((weights + 1, n)),
            dma((weights + 1, n)), dma((weights + 1, n)),
            dma((n,)), dma((n,)),
            dma((n, n)), dma((n, n)),
            dma((n, n, CORES)), dma((n, n_shard)),
            dma((n,)), dma((n,)),
            dma((2, n)), dma((2,)),
        ],
        compiler_params=pltpu.CompilerParams(
            collective_id=0, has_side_effects=True, vmem_limit_bytes=60 * 1024 * 1024
        ),
        name="towers",
    )(table_tower, table_owner, pool_view, down, up, comp, over_weight, cross_bias[0], comp_bias, over_bias)
    return result.reshape(1, block, out_width)


def solution(mesh):
    placed = (
        P("tower", None, "shard", None),
        P("tower", None, "shard", None),
        P("tower", None, None, "shard"),
        P("tower", None, None),
        P("tower", "shard", None),
        P("tower", None),
        P("tower", "shard"),
        P(),
        P(),
        P(),
    )
    towers, shards = mesh.shape["tower"], mesh.shape["shard"]
    body = turned if towers == SIDE * SIDE and towers * CORES == shards else on_device
    return jax.shard_map(
        body, mesh=mesh, in_specs=placed, out_specs=P("shard", "tower", None), check_vma=False
    )
```
